32 devices in a mesh: slab: 8 (over y, x, core), dom: 4 (over z).
Axes of the slice: x: 2, y: 2, z: 4, core: 2. Of those that a mesh axis runs over, the one named last changes fastest.
Arguments:
- rhs: float32 [6, 8, 6144], P(None, 'slab', 'dom'), may hold values from -6 to 6
- dshift: float32 [8, 6144], P('slab', 'dom'), may hold values from 0.5 to 4
- stiff: bfloat16 [8, 1024, 9216], P('slab', 'dom'), may hold values from -0.15625 to 0.15625
- face_k: bfloat16 [8, 2, 16, 9216], P('slab', None, 'dom'), may hold values from -0.625 to 0.625
- elem_col: int32 [8, 1024], P('slab', 'dom'), may hold values from 0 to 15
- elem_row: int32 [8, 1024], P('slab', 'dom'), may hold values from 0 to 63
- face_rows: int32 [8, 2], P('slab'), may hold values from 96 to 384, as said below
Outputs:
- solution: float32 [6, 8, 6144], P(None, 'slab', 'dom')
- residual: float32 [6, 8, 6144], P(None, 'slab', 'dom')
The draws below stay inside these ranges and needn't reach their ends.
Inputs may be any that keep to these rules, and one draw needn't show every extreme that they name: `face_rows`: in every draw one slab has a lower face with all 384 rows live.
All inputs are finite; a program needn't handle non-finite values.
Results may differ from the reference program's by a relative error of at most 0.0003.
Values sent between devices are 32-bit elements; how exact they have to be, the bound alone decides.
A program may use at most 64 MiB of HBM per device.

```python
import math
import jax
import jax.numpy as jnp
from jax import lax

BLOCK = 96
CASES = 6
ITERS = 2
RB_DEV = 16
EB_DEV = 256
FB_DEV = 4
SLAB_BLOCKS = 64
FACE_ROWS = 384
N_SLAB = 8
N_DOM = 4


def draw_face_rows(key, part):
    counts = jax.random.randint(key, (N_SLAB, 2), FACE_ROWS // 4, FACE_ROWS + 1)
    chosen = jax.random.randint(jax.random.fold_in(key, 7), (), 0, N_SLAB)
    return counts.at[chosen, 0].set(FACE_ROWS).astype(jnp.int32)


def set_ends(drawn, stream_key, least, top_value):
    index_at = [jax.random.randint(jax.random.fold_in(stream_key, axis), (), 0, length) for axis, length in enumerate(drawn.shape)]
    widest = drawn.shape.index(max(drawn.shape))
    beside = index_at[:widest] + [(index_at[widest] + 1) % drawn.shape[widest]] + index_at[widest + 1:]
    return drawn.at[tuple(index_at)].set(least).at[tuple(beside)].set(top_value)


def levels(own_key, shape, shards, least, high):
    loudness, own = 1.0, jax.random.fold_in(own_key, 6)
    for position, shards_of in shards:
        draws = jnp.exp(jax.random.uniform(jax.random.fold_in(own, position), (shards_of,), jnp.float32, least / len(shards), high / len(shards)))
        loudness = loudness * jnp.repeat(draws, shape[position] // shards_of).reshape([-1 if axis == position else 1 for axis in range(len(shape))])
    return loudness


def gaussian(rng, dims, scale, reach, split=(), held_as=jnp.bfloat16):
    drawn = scale * jax.random.normal(rng, dims, jnp.float32)
    if split:
        drawn = drawn * levels(rng, dims, split, -0.22, 0.18)
    return jnp.clip(drawn, -reach, reach).astype(held_as)


def setup_inputs(seed: int = 0) -> dict:
    arg_keys = jax.random.split(jax.random.key(seed), 8)
    rhs = gaussian(arg_keys[0], (CASES, N_SLAB, SLAB_BLOCKS * BLOCK), 1.0, 6.0, ((1, 8), (2, 4)), jnp.float32)
    dshift = jnp.clip(jnp.exp(math.log(4.0) - 2.0794415 * jax.random.uniform(arg_keys[1], (N_SLAB, SLAB_BLOCKS * BLOCK), jnp.float32) ** levels(arg_keys[1], (N_SLAB, SLAB_BLOCKS * BLOCK), ((0, 8), (1, 4)), -0.2, 0.2)), 0.5, 4.0)
    stiff = gaussian(arg_keys[2], (N_SLAB, N_DOM * EB_DEV, BLOCK * BLOCK), (BLOCK * EB_DEV // RB_DEV) ** -0.5, 0.15625, ((0, 8), (1, 4)))
    face_k = gaussian(arg_keys[3], (N_SLAB, 2, N_DOM * FB_DEV, BLOCK * BLOCK), BLOCK ** -0.5, 0.625, ((0, 8), (2, 4)))
    elem_col = set_ends(jax.random.randint(arg_keys[4], (N_SLAB, N_DOM * EB_DEV), 0, RB_DEV), jax.random.fold_in(arg_keys[4], 1), 0, RB_DEV - 1).astype(jnp.int32)
    elem_row = set_ends(jax.random.randint(arg_keys[5], (N_SLAB, N_DOM * EB_DEV), 0, SLAB_BLOCKS), jax.random.fold_in(arg_keys[5], 1), 0, SLAB_BLOCKS - 1).astype(jnp.int32)
    face_rows = draw_face_rows(jax.random.fold_in(arg_keys[7], 71), 0)
    return {"rhs": rhs, "dshift": dshift, "stiff": stiff, "face_k": face_k, "elem_col": elem_col, "elem_row": elem_row, "face_rows": face_rows}


highest = lax.Precision.HIGHEST


def slab_views(vector):
    leading = vector.shape[0]
    span = RB_DEV * BLOCK
    shaped = vector.reshape(leading, N_SLAB, N_DOM, span)
    lower = shaped[..., :FACE_ROWS].reshape(leading, N_SLAB, N_DOM, FB_DEV, BLOCK)
    upper = shaped[..., span - FACE_ROWS:].reshape(leading, N_SLAB, N_DOM, FB_DEV, BLOCK)
    return lower, upper


def add_faces(vector, lower_add, upper_add):
    leading = vector.shape[0]
    span = RB_DEV * BLOCK
    shaped = vector.reshape(leading, N_SLAB, N_DOM, span)
    shaped = shaped.at[..., :FACE_ROWS].add(lower_add.reshape(leading, N_SLAB, N_DOM, FACE_ROWS))
    shaped = shaped.at[..., span - FACE_ROWS:].add(upper_add.reshape(leading, N_SLAB, N_DOM, FACE_ROWS))
    return shaped.reshape(leading, N_SLAB, SLAB_BLOCKS * BLOCK)


def reference(rhs, dshift, stiff, face_k, elem_col, elem_row, face_rows):
    owner_base = (jnp.arange(N_DOM * EB_DEV, dtype=jnp.int32) // EB_DEV) * RB_DEV
    glob_cols = (elem_col + owner_base[None, :]).astype(jnp.int32)
    positions = jnp.arange(FACE_ROWS, dtype=jnp.int32)
    masks = (positions[None, None, :] < face_rows[:, :, None]).astype(jnp.float32)
    mask_low = masks[:, 0].reshape(1, N_SLAB, 1, FB_DEV, BLOCK)
    mask_up = masks[:, 1].reshape(1, N_SLAB, 1, FB_DEV, BLOCK)
    kface = face_k.astype(jnp.float32).reshape(N_SLAB, 2, N_DOM, FB_DEV, BLOCK, BLOCK)
    k_low = kface[:, 0]
    k_up = kface[:, 1]

    def intra_forward(items):
        blocks, columns, targets, vector = items
        matrices = blocks.astype(jnp.float32).reshape(-1, BLOCK, BLOCK)
        picked = vector.reshape(CASES, SLAB_BLOCKS, BLOCK)[:, columns]
        terms = jnp.einsum("gab,cgb->cga", matrices, picked, precision=highest)
        summed = jnp.zeros((CASES, SLAB_BLOCKS, BLOCK), jnp.float32).at[:, targets].add(terms)
        return summed.reshape(CASES, SLAB_BLOCKS * BLOCK)

    def intra_adjoint(items):
        blocks, columns, targets, vector = items
        matrices = blocks.astype(jnp.float32).reshape(-1, BLOCK, BLOCK)
        picked = vector.reshape(CASES, SLAB_BLOCKS, BLOCK)[:, targets]
        terms = jnp.einsum("gab,cga->cgb", matrices, picked, precision=highest)
        summed = jnp.zeros((CASES, SLAB_BLOCKS, BLOCK), jnp.float32).at[:, columns].add(terms)
        return summed.reshape(CASES, SLAB_BLOCKS * BLOCK)

    def per_slab(function, vector):
        result = lax.map(function, (stiff, glob_cols, elem_row, jnp.moveaxis(vector, 1, 0)))
        return jnp.moveaxis(result, 0, 1)

    def apply_operator(vector):
        lower, upper = slab_views(vector)
        from_below = jnp.roll(upper, 1, axis=1)
        from_above = jnp.roll(lower, -1, axis=1)
        term_low = jnp.einsum("sdiab,csdib->csdia", k_low, from_below, precision=highest) * mask_low
        term_up = jnp.einsum("sdiab,csdib->csdia", k_up, from_above, precision=highest) * mask_up
        image = add_faces(per_slab(intra_forward, vector), term_low, term_up)
        low_rows, up_rows = slab_views(image)
        back_low = jnp.einsum("sdiab,csdia->csdib", k_low, low_rows * mask_low, precision=highest)
        back_up = jnp.einsum("sdiab,csdia->csdib", k_up, up_rows * mask_up, precision=highest)
        adjoint = add_faces(per_slab(intra_adjoint, image), jnp.roll(back_up, 1, axis=1), jnp.roll(back_low, -1, axis=1))
        return dshift[None] * vector + adjoint

    def column_squares(items):
        blocks, columns = items
        matrices = blocks.astype(jnp.float32).reshape(-1, BLOCK, BLOCK)
        squares = jnp.sum(matrices * matrices, axis=1)
        summed = jnp.zeros((SLAB_BLOCKS, BLOCK), jnp.float32).at[columns].add(squares)
        return summed.reshape(SLAB_BLOCKS * BLOCK)

    inner = lax.map(column_squares, (stiff, glob_cols))
    sq_low = jnp.sum(k_low * k_low * mask_low[0][..., None], axis=3)
    sq_up = jnp.sum(k_up * k_up * mask_up[0][..., None], axis=3)
    diag_terms = add_faces(inner[None], jnp.roll(sq_up, 1, axis=0)[None], jnp.roll(sq_low, -1, axis=0)[None])
    inverse = 1.0 / (dshift[None] + diag_terms)

    def inner_product(first, second):
        return jnp.sum(first * second, axis=(1, 2))

    residual = rhs
    precond = inverse * residual
    direction = precond
    solution = jnp.zeros_like(rhs)
    rz_now = inner_product(residual, precond)
    for sweep in range(ITERS):
        image = apply_operator(direction)
        step_size = rz_now / inner_product(direction, image)
        solution = solution + step_size[:, None, None] * direction
        residual = residual - step_size[:, None, None] * image
        if sweep + 1 < ITERS:
            precond = inverse * residual
            rz_next = inner_product(residual, precond)
            direction = precond + (rz_next / rz_now)[:, None, None] * direction
            rz_now = rz_next
    return solution, residual
```

```python
import functools

import jax
import jax.numpy as jnp
from jax import lax
from jax.experimental import pallas as pl
from jax.experimental.pallas import tpu as pltpu
from jax.sharding import PartitionSpec as P

BLOCK = 96
LANES = 128
CASES = 6
ROWS = 8
ITERS = 2
CHUNK = 32
UNROLL = 32
SLOTS = 1
GROUP = 16
PAIRS = CASES // 2
MESH = pl.DeviceIdType.MESH
f32 = jnp.float32
bf16 = jnp.bfloat16


def split(x):
    high = x.astype(bf16).astype(f32)
    return jnp.concatenate([high, x - high], axis=0).astype(bf16)


def nn(a, b):
    return lax.dot_general(a, b, (((1,), (0,)), ((), ())), preferred_element_type=f32)


def nt(a, b):
    return lax.dot_general(a, b, (((1,), (1,)), ((), ())), preferred_element_type=f32)


def two(x):
    return x[:ROWS] + x[ROWS:]


def rows_of_four(tiles):
    t0, t1, t2 = tiles
    lane = lax.broadcasted_iota(jnp.int32, t0.shape, 1)
    live = lane < BLOCK
    zero = jnp.zeros_like(t0)
    roll = lambda t, n: pltpu.roll(t, n, 1)
    return (
        jnp.where(live, t0, zero),
        jnp.where(lane < 32, roll(t0, 32), jnp.where(live, roll(t1, 32), zero)),
        jnp.where(lane < 64, roll(t1, 64), jnp.where(live, roll(t2, 64), zero)),
        jnp.where(live, roll(t2, 96), zero),
    )


def four_as_three(rows):
    a, b, c, d = rows
    lane = lax.broadcasted_iota(jnp.int32, a.shape, 1)
    b, c, d = pltpu.roll(b, 96, 1), pltpu.roll(c, 64, 1), pltpu.roll(d, 32, 1)
    return jnp.where(lane < BLOCK, a, b), jnp.where(lane < 64, b, c), jnp.where(lane < 32, c, d)


def kernel(
    n_slab, n_dom,
    rhs_ref, dshift_ref, stiff_hbm, face_ref, col_s, row_s, col_v, row_v, rows_s,
    sol_ref, res_ref,
    sb, kt, perm, kb, kf, ys, sq, dg, wv, wr, terms, onehot_r, onehot_c, img,
    x_s, r_s, d_s, al_s, z_s, inv_s, dsh_s,
    sqf, rsqf, halo, part, rs, ag, back, rback, red,
    load_sem, sq_ss, sq_rs, halo_ss, halo_rs, rs_ss, rs_rs, ag_ss, ag_rs, bk_ss, bk_rs, rd_ss, rd_rs,
):
    E = stiff_hbm.shape[0]
    F = face_ref.shape[1]
    F2 = 2 * F
    J = rhs_ref.shape[2] // BLOCK
    R = J * n_dom
    EX = terms.shape[0]
    N = n_slab * n_dom
    slab = lax.axis_index("slab")
    dom = lax.axis_index("dom")
    lin = slab * n_dom + dom
    up = lax.rem(slab + 1, n_slab)
    down = lax.rem(slab + n_slab - 1, n_slab)

    def load_copy(i):
        rows = pl.ds(pl.multiple_of(i * CHUNK, CHUNK), CHUNK)
        return pltpu.make_async_copy(stiff_hbm.at[rows], sb.at[rows], load_sem.at[i])

    for i in range(E // CHUNK):
        load_copy(i).start()

    barrier = pltpu.get_barrier_semaphore()

    def greet(k, carry):
        other = lax.rem(lin + k, N)
        pl.semaphore_signal(
            barrier, inc=1, device_id=(other // n_dom, lax.rem(other, n_dom)), device_id_type=MESH
        )
        return carry

    lax.fori_loop(1, N, greet, 0)

    def exchange(src_low, src_up, dst, ss, rs_sem):
        return [
            pltpu.make_async_remote_copy(
                src_ref=src_up, dst_ref=dst.at[0], send_sem=ss.at[0], recv_sem=rs_sem.at[0],
                device_id=(up, dom), device_id_type=MESH,
            ),
            pltpu.make_async_remote_copy(
                src_ref=src_low, dst_ref=dst.at[1], send_sem=ss.at[1], recv_sem=rs_sem.at[1],
                device_id=(down, dom), device_id_type=MESH,
            ),
        ]

    e_id = lax.broadcasted_iota(jnp.int32, (F2, LANES), 0)
    limit = jnp.where(e_id < F, rows_s[0, 0] - e_id * BLOCK, rows_s[0, 1] - (e_id - F) * BLOCK)

    def aligned(at):
        return at if isinstance(at, int) else pl.multiple_of(at, LANES)

    def sixteen_rows(load, p, acc, store, mask=None, slot=0):
        count = acc.shape[0]
        for half in range(2):
            for quad in range(2):
                start = (p * 4 + half * 2 + quad) * 384
                tiles = [load(aligned(start + t * LANES)).astype(f32) for t in range(3)]
                for k, row in enumerate(rows_of_four(tiles)):
                    if mask is not None:
                        a = p * 16 + half * 8 + quad * 4 + k
                        row = jnp.where(mask > a, row, jnp.zeros_like(row))
                    acc = acc + row * row
                    for g in range(count // 8):
                        kt[slot, pl.ds((g * 2 + half) * 64 + quad * 4 + k, 8, stride=8), :] = row[g * 8 : g * 8 + 8]
        for g in range(count // 8):
            for e in range(8):
                pair = [kt[slot, pl.ds((g * 2 + half) * 64 + e * 8, 8), :] for half in range(2)]
                store(g * 8 + e, jnp.concatenate(pair, axis=0).astype(bf16))
        return acc

    def face_load(start):
        return jnp.concatenate([face_ref[0, :, pl.ds(start, LANES)], face_ref[1, :, pl.ds(start, LANES)]], axis=0)

    def face_step(p, acc):
        def store(e, tile):
            kf[e, pl.ds(pl.multiple_of(p * 16, 16), 16), :] = tile

        return sixteen_rows(lambda start: face_load(start).astype(f32), p, acc, store, limit)

    face_sq = lax.fori_loop(0, BLOCK // 16, face_step, jnp.zeros((F2, LANES), f32))
    sqf[0] = jnp.concatenate([face_sq[:F], jnp.zeros((ROWS - F, LANES), f32)], axis=0)
    sqf[1] = jnp.concatenate([face_sq[F:], jnp.zeros((ROWS - F, LANES), f32)], axis=0)

    pl.semaphore_wait(barrier, N - 1)
    sq_copies = exchange(sqf.at[0], sqf.at[1], rsqf, sq_ss, sq_rs)
    for c in sq_copies:
        c.start()

    r_s[...] = jnp.zeros(r_s.shape, f32)
    x_s[...] = jnp.zeros(x_s.shape, f32)
    dsh_s[...] = jnp.zeros(dsh_s.shape, f32)
    terms[...] = jnp.zeros(terms.shape, f32)
    ys[...] = jnp.zeros(ys.shape, f32)
    for j in range(J):
        for c in range(CASES):
            r_s[j, pl.ds(c, 1), pl.ds(0, BLOCK)] = rhs_ref[c, :, j * BLOCK : (j + 1) * BLOCK]
        dsh_s[pl.ds(j, 1), pl.ds(0, BLOCK)] = dshift_ref[:, j * BLOCK : (j + 1) * BLOCK]

    onehot_r[:, pl.ds(0, E)] = jnp.where(
        lax.broadcasted_iota(jnp.int32, (R, E), 0) == row_v[...], 1.0, 0.0
    ).astype(bf16)
    extra = lax.broadcasted_iota(jnp.int32, (R, EX - E), 1)
    aim = dom * J + jnp.where(extra < F, extra, extra + (J - F2))
    aim = jnp.where(extra < F2, aim, -1)
    onehot_r[:, pl.ds(E, EX - E)] = jnp.where(
        lax.broadcasted_iota(jnp.int32, (R, EX - E), 0) == aim, 1.0, 0.0
    ).astype(bf16)
    onehot_c[...] = jnp.where(
        lax.broadcasted_iota(jnp.int32, (J, E), 0) == col_v[...], 1.0, 0.0
    ).astype(bf16)

    i_out = lax.broadcasted_iota(jnp.int32, perm.shape, 0)
    i_in = lax.broadcasted_iota(jnp.int32, perm.shape, 1)
    perm[...] = jnp.where(i_out == (i_in % ROWS) * GROUP + i_in // ROWS, 1.0, 0.0).astype(bf16)

    def chunk_step(i, carry):
        load_copy(i).wait()
        base = pl.multiple_of(i * CHUNK, CHUNK)
        sums = [jnp.zeros((CHUNK, LANES), f32) for _ in range(3)]
        for p in range(BLOCK // GROUP):
            rows = []
            for q in range(GROUP // 4):
                start = (p * (GROUP // 4) + q) * 384
                tiles = [sb[pl.ds(base, CHUNK), pl.ds(start + t * LANES, LANES)].astype(f32) for t in range(3)]
                sums = [acc + w * w for acc, w in zip(sums, tiles)]
                rows += rows_of_four(tiles)
            for g in range(CHUNK // ROWS):
                picked = jnp.concatenate([row[g * ROWS : (g + 1) * ROWS] for row in rows], axis=0)
                turned = nn(perm[...], picked.astype(bf16)).astype(bf16)
                kb[pl.ds(base + g * ROWS, ROWS), pl.ds(p * GROUP, GROUP), :] = turned.reshape(ROWS, GROUP, LANES)
        sq[pl.ds(base, CHUNK), :] = sum(rows_of_four(sums))
        return carry

    lax.fori_loop(0, E // CHUNK, chunk_step, 0)

    sq_all = sq[...]
    sq_high = sq_all.astype(bf16)
    sq_low = (sq_all - sq_high.astype(f32)).astype(bf16)
    dg[...] = dsh_s[...] + nn(onehot_c[...], sq_high) + nn(onehot_c[...], sq_low)
    for c in sq_copies:
        c.wait()
    dg[pl.ds(0, F), :] += rsqf[0, pl.ds(0, F), :]
    dg[pl.ds(J - F, F), :] += rsqf[1, pl.ds(0, F), :]
    lane = lax.broadcasted_iota(jnp.int32, (J, LANES), 1)
    inv_s[...] = jnp.where(lane < BLOCK, 1.0 / jnp.where(lane < BLOCK, dg[...], 1.0), 0.0)

    blank = jnp.zeros((2 * ROWS, LANES), bf16)
    case_live = lax.broadcasted_iota(jnp.int32, (ROWS, 1), 0) < CASES
    rz_now = step_size = None

    for it in range(ITERS):
        rz_part = jnp.zeros((ROWS, LANES), f32)
        curv_part = jnp.zeros((ROWS, LANES), f32)
        for j in range(J):
            r_j = r_s[j]
            z_j = inv_s[pl.ds(j, 1), :] * r_j
            z_s[it, j] = z_j
            wv[j] = split(z_j)
            rz_part += r_j * z_j
            curv_part += dsh_s[pl.ds(j, 1), :] * z_j * z_j
        halo_copies = exchange(
            z_s.at[it, pl.ds(0, F)], z_s.at[it, pl.ds(J - F, F)], halo.at[it], halo_ss.at[it], halo_rs.at[it]
        )
        for c in halo_copies:
            c.start()

        def forward_step(s, carry):
            for u in range(UNROLL):
                e = s * UNROLL + u
                f = e + E // 2
                x_e = jnp.concatenate([wv[col_s[0, e]], blank], axis=1)
                x_f = jnp.concatenate([blank, wv[col_s[0, f]]], axis=1)
                y = nt(jnp.concatenate([x_e, x_f], axis=0), jnp.concatenate([kb[e], kb[f]], axis=1))
                terms[e, :, pl.ds(0, BLOCK)] = two(y[: 2 * ROWS])
                terms[f, :, pl.ds(0, BLOCK)] = two(y[2 * ROWS :])
            return carry

        lax.fori_loop(0, E // 2 // UNROLL, forward_step, 0)
        for c in halo_copies:
            c.wait()
        for k in range(2):
            for i in range(F):
                terms[E + k * F + i, :, pl.ds(0, BLOCK)] = two(nt(split(halo[it, k, i]), kf[k * F + i]))
        flat = terms.reshape(EX * ROWS, LANES)
        sel = onehot_r[...]
        H = J // 2
        rs_copies = []
        for m in range(PAIRS):
            quarters = []
            for c in (2 * m, 2 * m + 1):
                t_c = flat[pl.ds(c, EX, stride=ROWS), :]
                high = t_c.astype(bf16)
                low = (t_c - high.astype(f32)).astype(bf16)
                total = (nn(sel, high) + nn(sel, low)).reshape(n_dom, 2, H, LANES)
                quarters += [total[:, half].reshape(n_dom * H, LANES) for half in range(2)]
            for t, tile in enumerate(four_as_three(quarters)):
                part[it, m, :, t] = tile.reshape(n_dom, H, LANES)
            group = []
            for k in range(1, n_dom):
                other = lax.rem(dom + k, n_dom)
                c = pltpu.make_async_remote_copy(
                    src_ref=part.at[it, m, other], dst_ref=rs.at[it, m, k - 1],
                    send_sem=rs_ss.at[it, m, k - 1], recv_sem=rs_rs.at[it, m, k - 1],
                    device_id=(slab, other), device_id_type=MESH,
                )
                c.start()
                group.append(c)
            rs_copies.append(group)
        ag_copies = []
        for m in range(PAIRS):
            own = part[it, m, dom]
            for k in range(1, n_dom):
                rs_copies[m][k - 1].wait()
                own = own + rs[it, m, k - 1]
            ag[it, m, dom] = own
            group = []
            for k in range(1, n_dom):
                other = lax.rem(dom + k, n_dom)
                c = pltpu.make_async_remote_copy(
                    src_ref=ag.at[it, m, dom], dst_ref=ag.at[it, m, dom],
                    send_sem=ag_ss.at[it, m, k - 1], recv_sem=ag_rs.at[it, m, k - 1],
                    device_id=(slab, other), device_id_type=MESH,
                )
                c.start()
                group.append(c)
            ag_copies.append(group)

        def spread(owner, k, m):
            for t, tile in enumerate(rows_of_four([ag[it, m, owner, t] for t in range(3)])):
                ys[k, pl.ds((t % 2) * H * ROWS + 2 * m + t // 2, H, stride=ROWS), :] = tile

        def take_rows(owner, k):
            squares = jnp.zeros((ROWS, LANES), f32)
            for j in range(J):
                y = ys[k, pl.ds(j * ROWS, ROWS), :]
                wr[owner * J + j] = split(y)
                squares += y * y
            return squares

        for m in range(PAIRS):
            spread(dom, 0, m)
        curv_part += take_rows(dom, 0)
        lane8 = lax.broadcasted_iota(jnp.int32, (ROWS, LANES), 1)
        case8 = lax.broadcasted_iota(jnp.int32, (ROWS, LANES), 0)
        spot = jnp.where(lane8 == case8, jnp.sum(rz_part, axis=1, keepdims=True), 0.0) + jnp.where(
            lane8 == case8 + ROWS, jnp.sum(curv_part, axis=1, keepdims=True), 0.0
        )
        sums = jnp.sum(spot, axis=0, keepdims=True)
        red[it, lin] = sums

        def reduce_copy(k):
            other = lax.rem(lin + k, N)
            return pltpu.make_async_remote_copy(
                src_ref=red.at[it, lin], dst_ref=red.at[it, lin],
                send_sem=rd_ss.at[it, k], recv_sem=rd_rs.at[it, k],
                device_id=(other // n_dom, lax.rem(other, n_dom)), device_id_type=MESH,
            )

        def reduce_start(k, carry):
            reduce_copy(k).start()
            return carry

        def reduce_wait(k, carry):
            reduce_copy(k).wait()
            return carry

        for k in range(2):
            for i in range(F):
                back[it, k, i] = two(nn(wr[dom * J + (k * (J - F) + i), :, pl.ds(0, BLOCK)], kf[k * F + i]))
        back_copies = exchange(back.at[it, 0], back.at[it, 1], rback.at[it], bk_ss.at[it], bk_rs.at[it])
        for c in back_copies:
            c.start()
        lax.fori_loop(1, N, reduce_start, 0)
        for k in range(1, n_dom):
            owner = lax.rem(dom + n_dom - k, n_dom)
            for m in range(PAIRS):
                ag_copies[m][k - 1].wait()
                spread(owner, k, m)
            take_rows(owner, k)

        def adjoint_step(s, carry):
            for u in range(UNROLL):
                e = s * UNROLL + u
                f = e + E // 2
                y_e = wr[row_s[0, e], :, pl.ds(0, BLOCK)]
                y_f = wr[row_s[0, f], :, pl.ds(0, BLOCK)]
                x = nn(jnp.concatenate([y_e, y_f], axis=0), jnp.concatenate([kb[e], kb[f]], axis=1))
                terms[e] = two(x[: 2 * ROWS, :LANES])
                terms[f] = two(x[2 * ROWS :, LANES:])
            return carry

        lax.fori_loop(0, E // 2 // UNROLL, adjoint_step, 0)
        sel = onehot_c[...]
        img_flat = img.reshape(J * ROWS, LANES)
        for c in range(CASES):
            t_c = flat[pl.ds(c, E, stride=ROWS), :]
            high = t_c.astype(bf16)
            low = (t_c - high.astype(f32)).astype(bf16)
            img_flat[pl.ds(c, J, stride=ROWS), :] = nn(sel, high) + nn(sel, low)
        for c in back_copies:
            c.wait()
        lax.fori_loop(1, N, reduce_wait, 0)
        total = jnp.sum(red[it], axis=0)
        rz = jnp.sum(jnp.where(lane8 == case8, total, 0.0), axis=1, keepdims=True)
        curv = jnp.sum(jnp.where(lane8 == case8 + ROWS, total, 0.0), axis=1, keepdims=True)
        if it == 0:
            ratio = None
            step_size = jnp.where(case_live, rz / jnp.where(case_live, curv, 1.0), 0.0)
        else:
            ratio = jnp.where(case_live, rz / jnp.where(case_live, rz_now, 1.0), 0.0)
            bottom = curv - ratio * rz / jnp.where(case_live, step_size, 1.0)
            step_size = jnp.where(case_live, rz / jnp.where(case_live, bottom, 1.0), 0.0)
        rz_now = rz
        row_live = lax.broadcasted_iota(jnp.int32, (ROWS, LANES), 0) < CASES
        for j in range(J):
            z_j = z_s[it, j]
            y = jnp.where(row_live, img[j], 0.0) + dsh_s[pl.ds(j, 1), :] * z_j
            if j < F:
                y = y + rback[it, 0, j]
            if j >= J - F:
                y = y + rback[it, 1, j - (J - F)]
            if it == 0:
                d_j, a_j = z_j, y
            else:
                d_j = z_j + ratio * d_s[j]
                a_j = y + ratio * al_s[j]
            x_j = x_s[j] + step_size * d_j
            r_j = r_s[j] - step_size * a_j
            if it + 1 < ITERS:
                d_s[j] = d_j
                al_s[j] = a_j
            x_s[j] = x_j
            r_s[j] = r_j

    for source, target in ((x_s, sol_ref), (r_s, res_ref)):
        flat_out = jnp.concatenate([source[j, :, pl.ds(0, BLOCK)] for j in range(J)], axis=1)
        for c in range(CASES):
            target[c] = flat_out[c : c + 1]


def solution(mesh):
    n_slab, n_dom = mesh.shape["slab"], mesh.shape["dom"]
    N = n_slab * n_dom

    def body(rhs, dshift, stiff, face_k, elem_col, elem_row, face_rows):
        span = rhs.shape[2]
        J = span // BLOCK
        E = stiff.shape[1]
        F = face_k.shape[2]
        R = J * n_dom
        EX = E + 2 * ROWS
        H = J // 2
        vmem = pl.BlockSpec(memory_space=pltpu.VMEM)
        smem = pl.BlockSpec(memory_space=pltpu.SMEM)
        dma = pltpu.SemaphoreType.DMA
        out = pl.pallas_call(
            functools.partial(kernel, n_slab, n_dom),
            out_shape=(
                jax.ShapeDtypeStruct((CASES, 1, span), f32),
                jax.ShapeDtypeStruct((CASES, 1, span), f32),
            ),
            in_specs=[vmem, vmem, pl.BlockSpec(memory_space=pl.ANY), vmem, smem, smem, vmem, vmem, smem],
            out_specs=(vmem, vmem),
            scratch_shapes=[
                pltpu.VMEM((E, BLOCK * BLOCK), bf16),
                pltpu.VMEM((SLOTS, 2 * F * 16, LANES), f32),
                pltpu.VMEM((ROWS * GROUP, ROWS * GROUP), bf16),
                pltpu.VMEM((E, BLOCK, LANES), bf16),
                pltpu.VMEM((2 * F, BLOCK, LANES), bf16),
                pltpu.VMEM((n_dom, J * ROWS, LANES), f32),
                pltpu.VMEM((E, LANES), f32),
                pltpu.VMEM((J, LANES), f32),
                pltpu.VMEM((J, 2 * ROWS, LANES), bf16),
                pltpu.VMEM((R, 2 * ROWS, LANES), bf16),
                pltpu.VMEM((EX, ROWS, LANES), f32),
                pltpu.VMEM((R, EX), bf16),
                pltpu.VMEM((J, E), bf16),
                pltpu.VMEM((J, ROWS, LANES), f32),
                pltpu.VMEM((J, ROWS, LANES), f32),
                pltpu.VMEM((J, ROWS, LANES), f32),
                pltpu.VMEM((J, ROWS, LANES), f32),
                pltpu.VMEM((J, ROWS, LANES), f32),
                pltpu.VMEM((ITERS, J, ROWS, LANES), f32),
                pltpu.VMEM((J, LANES), f32),
                pltpu.VMEM((J, LANES), f32),
                pltpu.VMEM((2, ROWS, LANES), f32),
                pltpu.VMEM((2, ROWS, LANES), f32),
                pltpu.VMEM((ITERS, 2, F, ROWS, LANES), f32),
                pltpu.VMEM((ITERS, PAIRS, n_dom, 3, H, LANES), f32),
                pltpu.VMEM((ITERS, PAIRS, n_dom - 1, 3, H, LANES), f32),
                pltpu.VMEM((ITERS, PAIRS, n_dom, 3, H, LANES), f32),
                pltpu.VMEM((ITERS, 2, F, ROWS, LANES), f32),
                pltpu.VMEM((ITERS, 2, F, ROWS, LANES), f32),
                pltpu.VMEM((ITERS, N, 1, LANES), f32),
                dma((E // CHUNK,)),
                dma((2,)),
                dma((2,)),
                dma((ITERS, 2)),
                dma((ITERS, 2)),
                dma((ITERS, PAIRS, n_dom - 1)),
                dma((ITERS, PAIRS, n_dom - 1)),
                dma((ITERS, PAIRS, n_dom - 1)),
                dma((ITERS, PAIRS, n_dom - 1)),
                dma((ITERS, 2)),
                dma((ITERS, 2)),
                dma((ITERS, N)),
                dma((ITERS, N)),
            ],
            compiler_params=pltpu.CompilerParams(
                collective_id=0, has_side_effects=True, vmem_limit_bytes=56 * 1024 * 1024
            ),
        )(
            rhs, dshift, stiff.reshape(E, BLOCK * BLOCK),
            face_k.reshape(2, F, BLOCK * BLOCK), elem_col, elem_row, elem_col, elem_row, face_rows,
        )
        return out

    return jax.shard_map(
        body,
        mesh=mesh,
        in_specs=(
            P(None, "slab", "dom"),
            P("slab", "dom"),
            P("slab", "dom", None),
            P("slab", None, "dom", None),
            P("slab", "dom"),
            P("slab", "dom"),
            P("slab", None),
        ),
        out_specs=(P(None, "slab", "dom"), P(None, "slab", "dom")),
        check_vma=False,
    )
```

```python
import functools

import jax
import jax.numpy as jnp
from jax import lax
from jax.experimental import pallas as pl
from jax.experimental.pallas import tpu as pltpu
from jax.sharding import PartitionSpec as P

BLOCK = 96
LANES = 128
CASES = 6
ROWS = 8
ITERS = 2
CHUNK = 32
UNROLL = 64
SLOTS = 1
GROUP = 16
PART = 32
PARTS = BLOCK // PART
MESH = pl.DeviceIdType.MESH
f32 = jnp.float32
bf16 = jnp.bfloat16


def split(x):
    high = x.astype(bf16).astype(f32)
    return jnp.concatenate([high, x - high], axis=0).astype(bf16)


def nn(a, b):
    return lax.dot_general(a, b, (((1,), (0,)), ((), ())), preferred_element_type=f32)


def nt(a, b):
    return lax.dot_general(a, b, (((1,), (1,)), ((), ())), preferred_element_type=f32)


def two(x):
    return x[:ROWS] + x[ROWS:]


def rows_of_four(tiles):
    t0, t1, t2 = tiles
    lane = lax.broadcasted_iota(jnp.int32, t0.shape, 1)
    live = lane < BLOCK
    zero = jnp.zeros_like(t0)
    roll = lambda t, n: pltpu.roll(t, n, 1)
    return (
        jnp.where(live, t0, zero),
        jnp.where(lane < 32, roll(t0, 32), jnp.where(live, roll(t1, 32), zero)),
        jnp.where(lane < 64, roll(t1, 64), jnp.where(live, roll(t2, 64), zero)),
        jnp.where(live, roll(t2, 96), zero),
    )


def turn(x, shift):
    shift %= LANES
    return pltpu.roll(x, shift, 1) if shift else x


def lay(pieces):
    lane = lax.broadcasted_iota(jnp.int32, pieces[0][0].shape, 1)
    out = jnp.zeros_like(pieces[0][0]) if len(pieces) * PART < LANES else None
    for n in reversed(range(len(pieces))):
        tile, start = pieces[n]
        tile = turn(tile, n * PART - start)
        out = tile if out is None else jnp.where(lane < (n + 1) * PART, tile, out)
    return out


def by_case(ref, c):
    n = ref.shape[0]
    return ref.reshape(n * ROWS, LANES)[pl.ds(c, n, stride=ROWS), :]


def kernel(
    n_slab, n_dom,
    rhs_ref, dshift_ref, stiff_hbm, face_ref, col_s, row_s, col_v, row_v, rows_s,
    sol_ref, res_ref,
    sb, kt, perm, kb, kf, ya, yb, sq, dg, wv, wa, wb, terms, ta, tb, fadd, onehot_r, onehot_c, img,
    x_s, r_s, d_s, al_s, z_s, inv_s, dsh_s,
    sqf, rsqf, halo, part, rs, ag, back, rback, red,
    load_sem, sq_ss, sq_rs, halo_ss, halo_rs, rs_ss, rs_rs, ag_ss, ag_rs, bk_ss, bk_rs, rd_ss, rd_rs,
):
    E = stiff_hbm.shape[0]
    F = face_ref.shape[1]
    F2 = 2 * F
    J = rhs_ref.shape[2] // BLOCK
    R = J * n_dom
    H = J // 2
    N = n_slab * n_dom
    slab = lax.axis_index("slab")
    dom = lax.axis_index("dom")
    lin = slab * n_dom + dom
    up = lax.rem(slab + 1, n_slab)
    down = lax.rem(slab + n_slab - 1, n_slab)

    def load_copy(i):
        rows = pl.ds(pl.multiple_of(i * CHUNK, CHUNK), CHUNK)
        return pltpu.make_async_copy(stiff_hbm.at[rows], sb.at[rows], load_sem.at[i])

    for i in range(E // CHUNK):
        load_copy(i).start()

    barrier = pltpu.get_barrier_semaphore()

    def greet(k, carry):
        other = lax.rem(lin + k, N)
        pl.semaphore_signal(
            barrier, inc=1, device_id=(other // n_dom, lax.rem(other, n_dom)), device_id_type=MESH
        )
        return carry

    lax.fori_loop(1, N, greet, 0)

    def exchange(src_low, src_up, dst, ss, rs_sem):
        return [
            pltpu.make_async_remote_copy(
                src_ref=src_up, dst_ref=dst.at[0], send_sem=ss.at[0], recv_sem=rs_sem.at[0],
                device_id=(up, dom), device_id_type=MESH,
            ),
            pltpu.make_async_remote_copy(
                src_ref=src_low, dst_ref=dst.at[1], send_sem=ss.at[1], recv_sem=rs_sem.at[1],
                device_id=(down, dom), device_id_type=MESH,
            ),
        ]

    e_id = lax.broadcasted_iota(jnp.int32, (F2, LANES), 0)
    limit = jnp.where(e_id < F, rows_s[0, 0] - e_id * BLOCK, rows_s[0, 1] - (e_id - F) * BLOCK)

    def aligned(at):
        return at if isinstance(at, int) else pl.multiple_of(at, LANES)

    def sixteen_rows(load, p, acc, store, mask=None, slot=0):
        count = acc.shape[0]
        for half in range(2):
            for quad in range(2):
                start = (p * 4 + half * 2 + quad) * 384
                tiles = [load(aligned(start + t * LANES)).astype(f32) for t in range(3)]
                for k, row in enumerate(rows_of_four(tiles)):
                    if mask is not None:
                        a = p * 16 + half * 8 + quad * 4 + k
                        row = jnp.where(mask > a, row, jnp.zeros_like(row))
                    acc = acc + row * row
                    for g in range(count // 8):
                        kt[slot, pl.ds((g * 2 + half) * 64 + quad * 4 + k, 8, stride=8), :] = row[g * 8 : g * 8 + 8]
        for g in range(count // 8):
            for e in range(8):
                pair = [kt[slot, pl.ds((g * 2 + half) * 64 + e * 8, 8), :] for half in range(2)]
                store(g * 8 + e, jnp.concatenate(pair, axis=0).astype(bf16))
        return acc

    def face_load(start):
        return jnp.concatenate([face_ref[0, :, pl.ds(start, LANES)], face_ref[1, :, pl.ds(start, LANES)]], axis=0)

    def face_step(p, acc):
        def store(e, tile):
            kf[e, pl.ds(pl.multiple_of(p * 16, 16), 16), :] = tile

        return sixteen_rows(lambda start: face_load(start).astype(f32), p, acc, store, limit)

    face_sq = lax.fori_loop(0, BLOCK // 16, face_step, jnp.zeros((F2, LANES), f32))
    sqf[0] = jnp.concatenate([face_sq[:F], jnp.zeros((ROWS - F, LANES), f32)], axis=0)
    sqf[1] = jnp.concatenate([face_sq[F:], jnp.zeros((ROWS - F, LANES), f32)], axis=0)

    pl.semaphore_wait(barrier, N - 1)
    sq_copies = exchange(sqf.at[0], sqf.at[1], rsqf, sq_ss, sq_rs)
    for c in sq_copies:
        c.start()

    r_s[...] = jnp.zeros(r_s.shape, f32)
    x_s[...] = jnp.zeros(x_s.shape, f32)
    dsh_s[...] = jnp.zeros(dsh_s.shape, f32)
    fadd[...] = jnp.zeros(fadd.shape, f32)
    ya[...] = jnp.zeros(ya.shape, f32)
    yb[...] = jnp.zeros(yb.shape, f32)
    for j in range(J):
        for c in range(CASES):
            r_s[j, pl.ds(c, 1), pl.ds(0, BLOCK)] = rhs_ref[c, :, j * BLOCK : (j + 1) * BLOCK]
        dsh_s[pl.ds(j, 1), pl.ds(0, BLOCK)] = dshift_ref[:, j * BLOCK : (j + 1) * BLOCK]

    onehot_r[...] = jnp.where(
        lax.broadcasted_iota(jnp.int32, (R, E), 0) == row_v[...], 1.0, 0.0
    ).astype(bf16)
    onehot_c[...] = jnp.where(
        lax.broadcasted_iota(jnp.int32, (J, E), 0) == col_v[...], 1.0, 0.0
    ).astype(bf16)

    i_out = lax.broadcasted_iota(jnp.int32, perm.shape, 0)
    i_in = lax.broadcasted_iota(jnp.int32, perm.shape, 1)
    perm[...] = jnp.where(i_out == (i_in % ROWS) * GROUP + i_in // ROWS, 1.0, 0.0).astype(bf16)

    def chunk_step(i, carry):
        load_copy(i).wait()
        base = pl.multiple_of(i * CHUNK, CHUNK)
        sums = [jnp.zeros((CHUNK, LANES), f32) for _ in range(3)]
        for p in range(BLOCK // GROUP):
            rows = []
            for q in range(GROUP // 4):
                start = (p * (GROUP // 4) + q) * 384
                tiles = [sb[pl.ds(base, CHUNK), pl.ds(start + t * LANES, LANES)].astype(f32) for t in range(3)]
                sums = [acc + w * w for acc, w in zip(sums, tiles)]
                rows += rows_of_four(tiles)
            for g in range(CHUNK // ROWS):
                picked = jnp.concatenate([row[g * ROWS : (g + 1) * ROWS] for row in rows], axis=0)
                turned = nn(perm[...], picked.astype(bf16)).astype(bf16)
                kb[pl.ds(base + g * ROWS, ROWS), pl.ds(p * GROUP, GROUP), :] = turned.reshape(ROWS, GROUP, LANES)
        sq[pl.ds(base, CHUNK), :] = sum(rows_of_four(sums))
        return carry

    lax.fori_loop(0, E // CHUNK, chunk_step, 0)

    sq_all = sq[...]
    sq_high = sq_all.astype(bf16)
    sq_low = (sq_all - sq_high.astype(f32)).astype(bf16)
    dg[...] = dsh_s[...] + nn(onehot_c[...], sq_high) + nn(onehot_c[...], sq_low)
    for c in sq_copies:
        c.wait()
    dg[pl.ds(0, F), :] += rsqf[0, pl.ds(0, F), :]
    dg[pl.ds(J - F, F), :] += rsqf[1, pl.ds(0, F), :]
    lane = lax.broadcasted_iota(jnp.int32, (J, LANES), 1)
    inv_s[...] = jnp.where(lane < BLOCK, 1.0 / jnp.where(lane < BLOCK, dg[...], 1.0), 0.0)

    blank = jnp.zeros((2 * ROWS, LANES), bf16)
    case_live = lax.broadcasted_iota(jnp.int32, (ROWS, 1), 0) < CASES
    rz_now = step_size = None

    for it in range(ITERS):
        rz_part = jnp.zeros((ROWS, LANES), f32)
        curv_part = jnp.zeros((ROWS, LANES), f32)
        for j in range(J):
            r_j = r_s[j]
            z_j = inv_s[pl.ds(j, 1), :] * r_j
            z_s[it, j] = z_j
            wv[j] = split(z_j)
            rz_part += r_j * z_j
            curv_part += dsh_s[pl.ds(j, 1), :] * z_j * z_j
        halo_copies = exchange(
            z_s.at[it, pl.ds(0, F)], z_s.at[it, pl.ds(J - F, F)], halo.at[it], halo_ss.at[it], halo_rs.at[it]
        )
        for c in halo_copies:
            c.start()

        rs_copies, ag_copies = [], []
        for h in range(PARTS):
            rows_h = pl.ds(h * PART, PART)

            def forward_step(s, carry):
                for u in range(UNROLL):
                    e = s * UNROLL + u
                    f = e + E // 2
                    x_e = jnp.concatenate([wv[col_s[0, e]], blank], axis=1)
                    x_f = jnp.concatenate([blank, wv[col_s[0, f]]], axis=1)
                    k_ef = jnp.concatenate([kb[e, rows_h], kb[f, rows_h]], axis=1)
                    y = nt(jnp.concatenate([x_e, x_f], axis=0), k_ef)
                    terms[e, :, pl.ds(0, PART)] = two(y[: 2 * ROWS])
                    terms[f, :, pl.ds(0, PART)] = two(y[2 * ROWS :])
                return carry

            lax.fori_loop(0, E // 2 // UNROLL, forward_step, 0)
            t = [by_case(terms, c) for c in range(CASES)]
            packed = jnp.concatenate([lay([(x, 0) for x in t[:4]]), lay([(x, 0) for x in t[4:]])], axis=1)
            high = packed.astype(bf16)
            low = (packed - high.astype(f32)).astype(bf16)
            total = nn(onehot_r[...], high) + nn(onehot_r[...], low)
            part[it, h, :, pl.ds(0, J)] = total[:, :LANES].reshape(n_dom, J, LANES)
            rest = total[:, LANES:].reshape(n_dom, 2, H, LANES)
            first, second = (rest[:, half].reshape(n_dom * H, LANES) for half in range(2))
            first = jnp.where(lax.broadcasted_iota(jnp.int32, first.shape, 1) < 2 * PART, first, turn(second, 2 * PART))
            part[it, h, :, pl.ds(J, H)] = first.reshape(n_dom, H, LANES)
            group = []
            for k in range(1, n_dom):
                other = lax.rem(dom + k, n_dom)
                c = pltpu.make_async_remote_copy(
                    src_ref=part.at[it, h, other], dst_ref=rs.at[it, h, k - 1],
                    send_sem=rs_ss.at[it, h, k - 1], recv_sem=rs_rs.at[it, h, k - 1],
                    device_id=(slab, other), device_id_type=MESH,
                )
                c.start()
                group.append(c)
            rs_copies.append(group)

        for c in halo_copies:
            c.wait()
        for k in range(2):
            for i in range(F):
                j = k * (J - F) + i
                fadd[j, :, pl.ds(0, BLOCK)] = two(nt(split(halo[it, k, i]), kf[k * F + i]))
        face_parts = []
        for h in range(PARTS):
            t = [by_case(fadd, c) for c in range(CASES)]
            face_parts.append((
                lay([(x, h * PART) for x in t[:4]]),
                lay([(x[half * H : half * H + H], h * PART) for half in range(2) for x in t[4:]]),
            ))

        for h in range(PARTS):
            own = part[it, h, dom] + jnp.concatenate(face_parts[h], axis=0)
            for k in range(1, n_dom):
                rs_copies[h][k - 1].wait()
                own = own + rs[it, h, k - 1]
            ag[it, h, dom] = own
            group = []
            for k in range(1, n_dom):
                other = lax.rem(dom + k, n_dom)
                c = pltpu.make_async_remote_copy(
                    src_ref=ag.at[it, h, dom], dst_ref=ag.at[it, h, dom],
                    send_sem=ag_ss.at[it, h, k - 1], recv_sem=ag_rs.at[it, h, k - 1],
                    device_id=(slab, other), device_id_type=MESH,
                )
                c.start()
                group.append(c)
            ag_copies.append(group)

        def spread(owner, slot, parts, dst):
            for half in range(2):
                for c in range(CASES):
                    if c < 4:
                        where, start = pl.ds(half * H, H), c * PART
                    else:
                        where, start = pl.ds(J, H), (2 * half + c - 4) * PART
                    tile = lay([(ag[it, h, owner, where], start) for h in parts])
                    dst[slot, pl.ds(half * H * ROWS + c, H, stride=ROWS), :] = tile

        def take_rows(owner, slot, src, dst):
            squares = jnp.zeros((ROWS, LANES), f32)
            for j in range(J):
                y = src[slot, pl.ds(j * ROWS, ROWS), :]
                dst[owner * J + j] = split(y)
                squares += y * y
            return squares

        a_parts, b_parts = tuple(range(PARTS - 1)), (PARTS - 1,)
        spread(dom, 0, a_parts, ya)
        spread(dom, 0, b_parts, yb)
        curv_part += take_rows(dom, 0, ya, wa) + take_rows(dom, 0, yb, wb)
        lane8 = lax.broadcasted_iota(jnp.int32, (ROWS, LANES), 1)
        case8 = lax.broadcasted_iota(jnp.int32, (ROWS, LANES), 0)
        spot = jnp.where(lane8 == case8, jnp.sum(rz_part, axis=1, keepdims=True), 0.0) + jnp.where(
            lane8 == case8 + ROWS, jnp.sum(curv_part, axis=1, keepdims=True), 0.0
        )
        sums = jnp.sum(spot, axis=0, keepdims=True)
        red[it, lin] = sums

        def reduce_copy(k):
            other = lax.rem(lin + k, N)
            return pltpu.make_async_remote_copy(
                src_ref=red.at[it, lin], dst_ref=red.at[it, lin],
                send_sem=rd_ss.at[it, k], recv_sem=rd_rs.at[it, k],
                device_id=(other // n_dom, lax.rem(other, n_dom)), device_id_type=MESH,
            )

        def reduce_start(k, carry):
            reduce_copy(k).start()
            return carry

        def reduce_wait(k, carry):
            reduce_copy(k).wait()
            return carry

        lax.fori_loop(1, N, reduce_start, 0)
        for k in range(2):
            for i in range(F):
                row = dom * J + (k * (J - F) + i)
                back[it, k, i] = two(
                    nn(wa[row, :, pl.ds(0, BLOCK - PART)], kf[k * F + i, pl.ds(0, BLOCK - PART)])
                    + nn(wb[row, :, pl.ds(0, PART)], kf[k * F + i, pl.ds(BLOCK - PART, PART)])
                )
        back_copies = exchange(back.at[it, 0], back.at[it, 1], rback.at[it], bk_ss.at[it], bk_rs.at[it])
        for c in back_copies:
            c.start()

        for parts, y_buf, w_buf, t_buf in ((a_parts, ya, wa, ta), (b_parts, yb, wb, tb)):
            for k in range(1, n_dom):
                owner = lax.rem(dom + n_dom - k, n_dom)
                for h in parts:
                    ag_copies[h][k - 1].wait()
                spread(owner, k, parts, y_buf)
                take_rows(owner, k, y_buf, w_buf)
            wide = len(parts) * PART
            rows_p = pl.ds(parts[0] * PART, wide)

            def adjoint_step(s, carry):
                for u in range(UNROLL):
                    e = s * UNROLL + u
                    f = e + E // 2
                    y_e = w_buf[row_s[0, e], :, pl.ds(0, wide)]
                    y_f = w_buf[row_s[0, f], :, pl.ds(0, wide)]
                    k_ef = jnp.concatenate([kb[e, rows_p], kb[f, rows_p]], axis=1)
                    x = nn(jnp.concatenate([y_e, y_f], axis=0), k_ef)
                    t_buf[e] = two(x[: 2 * ROWS, :LANES])
                    t_buf[f] = two(x[2 * ROWS :, LANES:])
                return carry

            lax.fori_loop(0, E // 2 // UNROLL, adjoint_step, 0)
        sel = onehot_c[...]
        img_flat = img.reshape(J * ROWS, LANES)
        for m in range(CASES // 2):
            t = [by_case(ta, c) + by_case(tb, c) for c in (2 * m, 2 * m + 1)]
            t = jnp.concatenate(t, axis=1)
            high = t.astype(bf16)
            low = (t - high.astype(f32)).astype(bf16)
            total = nn(sel, high) + nn(sel, low)
            for k in range(2):
                img_flat[pl.ds(2 * m + k, J, stride=ROWS), :] = total[:, k * LANES : (k + 1) * LANES]
        for c in back_copies:
            c.wait()
        lax.fori_loop(1, N, reduce_wait, 0)
        total = jnp.sum(red[it], axis=0)
        rz = jnp.sum(jnp.where(lane8 == case8, total, 0.0), axis=1, keepdims=True)
        curv = jnp.sum(jnp.where(lane8 == case8 + ROWS, total, 0.0), axis=1, keepdims=True)
        if it == 0:
            ratio = None
            step_size = jnp.where(case_live, rz / jnp.where(case_live, curv, 1.0), 0.0)
        else:
            ratio = jnp.where(case_live, rz / jnp.where(case_live, rz_now, 1.0), 0.0)
            bottom = curv - ratio * rz / jnp.where(case_live, step_size, 1.0)
            step_size = jnp.where(case_live, rz / jnp.where(case_live, bottom, 1.0), 0.0)
        rz_now = rz
        row_live = lax.broadcasted_iota(jnp.int32, (ROWS, LANES), 0) < CASES
        for j in range(J):
            z_j = z_s[it, j]
            y = jnp.where(row_live, img[j], 0.0) + dsh_s[pl.ds(j, 1), :] * z_j
            if j < F:
                y = y + rback[it, 0, j]
            if j >= J - F:
                y = y + rback[it, 1, j - (J - F)]
            if it == 0:
                d_j, a_j = z_j, y
            else:
                d_j = z_j + ratio * d_s[j]
                a_j = y + ratio * al_s[j]
            x_j = x_s[j] + step_size * d_j
            r_j = r_s[j] - step_size * a_j
            if it + 1 < ITERS:
                d_s[j] = d_j
                al_s[j] = a_j
            x_s[j] = x_j
            r_s[j] = r_j

    for source, target in ((x_s, sol_ref), (r_s, res_ref)):
        flat_out = jnp.concatenate([source[j, :, pl.ds(0, BLOCK)] for j in range(J)], axis=1)
        for c in range(CASES):
            target[c] = flat_out[c : c + 1]


def solution(mesh):
    n_slab, n_dom = mesh.shape["slab"], mesh.shape["dom"]
    N = n_slab * n_dom

    def body(rhs, dshift, stiff, face_k, elem_col, elem_row, face_rows):
        span = rhs.shape[2]
        J = span // BLOCK
        E = stiff.shape[1]
        F = face_k.shape[2]
        R = J * n_dom
        H = J // 2
        vmem = pl.BlockSpec(memory_space=pltpu.VMEM)
        smem = pl.BlockSpec(memory_space=pltpu.SMEM)
        dma = pltpu.SemaphoreType.DMA
        out = pl.pallas_call(
            functools.partial(kernel, n_slab, n_dom),
            out_shape=(
                jax.ShapeDtypeStruct((CASES, 1, span), f32),
                jax.ShapeDtypeStruct((CASES, 1, span), f32),
            ),
            in_specs=[vmem, vmem, pl.BlockSpec(memory_space=pl.ANY), vmem, smem, smem, vmem, vmem, smem],
            out_specs=(vmem, vmem),
            scratch_shapes=[
                pltpu.VMEM((E, BLOCK * BLOCK), bf16),
                pltpu.VMEM((SLOTS, 2 * F * 16, LANES), f32),
                pltpu.VMEM((ROWS * GROUP, ROWS * GROUP), bf16),
                pltpu.VMEM((E, BLOCK, LANES), bf16),
                pltpu.VMEM((2 * F, BLOCK, LANES), bf16),
                pltpu.VMEM((n_dom, J * ROWS, LANES), f32),
                pltpu.VMEM((n_dom, J * ROWS, LANES), f32),
                pltpu.VMEM((E, LANES), f32),
                pltpu.VMEM((J, LANES), f32),
                pltpu.VMEM((J, 2 * ROWS, LANES), bf16),
                pltpu.VMEM((R, 2 * ROWS, LANES), bf16),
                pltpu.VMEM((R, 2 * ROWS, LANES), bf16),
                pltpu.VMEM((E, ROWS, LANES), f32),
                pltpu.VMEM((E, ROWS, LANES), f32),
                pltpu.VMEM((E, ROWS, LANES), f32),
                pltpu.VMEM((J, ROWS, LANES), f32),
                pltpu.VMEM((R, E), bf16),
                pltpu.VMEM((J, E), bf16),
                pltpu.VMEM((J, ROWS, LANES), f32),
                pltpu.VMEM((J, ROWS, LANES), f32),
                pltpu.VMEM((J, ROWS, LANES), f32),
                pltpu.VMEM((J, ROWS, LANES), f32),
                pltpu.VMEM((J, ROWS, LANES), f32),
                pltpu.VMEM((ITERS, J, ROWS, LANES), f32),
                pltpu.VMEM((J, LANES), f32),
                pltpu.VMEM((J, LANES), f32),
                pltpu.VMEM((2, ROWS, LANES), f32),
                pltpu.VMEM((2, ROWS, LANES), f32),
                pltpu.VMEM((ITERS, 2, F, ROWS, LANES), f32),
                pltpu.VMEM((ITERS, PARTS, n_dom, J + H, LANES), f32),
                pltpu.VMEM((ITERS, PARTS, n_dom - 1, J + H, LANES), f32),
                pltpu.VMEM((ITERS, PARTS, n_dom, J + H, LANES), f32),
                pltpu.VMEM((ITERS, 2, F, ROWS, LANES), f32),
                pltpu.VMEM((ITERS, 2, F, ROWS, LANES), f32),
                pltpu.VMEM((ITERS, N, 1, LANES), f32),
                dma((E // CHUNK,)),
                dma((2,)),
                dma((2,)),
                dma((ITERS, 2)),
                dma((ITERS, 2)),
                dma((ITERS, PARTS, n_dom - 1)),
                dma((ITERS, PARTS, n_dom - 1)),
                dma((ITERS, PARTS, n_dom - 1)),
                dma((ITERS, PARTS, n_dom - 1)),
                dma((ITERS, 2)),
                dma((ITERS, 2)),
                dma((ITERS, N)),
                dma((ITERS, N)),
            ],
            compiler_params=pltpu.CompilerParams(
                collective_id=0, has_side_effects=True, vmem_limit_bytes=56 * 1024 * 1024
            ),
        )(
            rhs, dshift, stiff.reshape(E, BLOCK * BLOCK),
            face_k.reshape(2, F, BLOCK * BLOCK), elem_col, elem_row, elem_col, elem_row, face_rows,
        )
        return out

    return jax.shard_map(
        body,
        mesh=mesh,
        in_specs=(
            P(None, "slab", "dom"),
            P("slab", "dom"),
            P("slab", "dom", None),
            P("slab", None, "dom", None),
            P("slab", "dom"),
            P("slab", "dom"),
            P("slab", None),
        ),
        out_specs=(P(None, "slab", "dom"), P(None, "slab", "dom")),
        check_vma=False,
    )
```

```python
import functools

import jax
import jax.numpy as jnp
from jax import lax
from jax.experimental import pallas as pl
from jax.experimental.pallas import tpu as pltpu
from jax.sharding import PartitionSpec as P

BLOCK = 96
LANES = 128
CASES = 6
ROWS = 8
ITERS = 2
CHUNK = 128
UNROLL = 128
SLOTS = 1
GROUP = 16
PART = 32
PARTS = BLOCK // PART
MESH = pl.DeviceIdType.MESH
f32 = jnp.float32
bf16 = jnp.bfloat16


def split(x):
    high = x.astype(bf16).astype(f32)
    return jnp.concatenate([high, x - high], axis=0).astype(bf16)


def nn(a, b):
    return lax.dot_general(a, b, (((1,), (0,)), ((), ())), preferred_element_type=f32)


def nt(a, b):
    return lax.dot_general(a, b, (((1,), (1,)), ((), ())), preferred_element_type=f32)


def two(x):
    return x[:ROWS] + x[ROWS:]


def rows_of_four(tiles):
    t0, t1, t2 = tiles
    lane = lax.broadcasted_iota(jnp.int32, t0.shape, 1)
    return (
        t0,
        jnp.where(lane < 32, turn(t0, 32), turn(t1, 32)),
        jnp.where(lane < 64, turn(t1, 64), turn(t2, 64)),
        turn(t2, 96),
    )


def turn(x, shift):
    shift %= LANES
    return pltpu.roll(x, shift, 1) if shift else x


def lay(pieces):
    lane = lax.broadcasted_iota(jnp.int32, pieces[0][0].shape, 1)
    out = jnp.zeros_like(pieces[0][0]) if len(pieces) * PART < LANES else None
    for n in reversed(range(len(pieces))):
        tile, start = pieces[n]
        tile = turn(tile, n * PART - start)
        out = tile if out is None else jnp.where(lane < (n + 1) * PART, tile, out)
    return out


def by_case(ref, c):
    return ref[:, c].reshape(ref.shape[0] * ROWS, LANES)


def halves(ref):
    n = ref.shape[0] // 2
    return ref.at[pl.ds(0, n)], ref.at[pl.ds(n, n)]


def term_rows(ref, s, u):
    at = (s * (UNROLL // ROWS) + u // ROWS) * ROWS * ROWS + u % ROWS
    return ref.reshape(ref.shape[0] * ROWS * ROWS, LANES), pl.ds(at, ROWS, stride=ROWS)


def wait_bytes(ref, sem):
    pltpu.make_async_copy(ref, ref, sem).wait()


def steps(count, step):
    if count == 1:
        step(0, 0)
    else:
        lax.fori_loop(0, count, step, 0)


def kernel(
    n_slab, n_dom,
    rhs_hbm, dshift_hbm, stiff_hbm, face_hbm, col_hbm, row_hbm, rows_hbm,
    sol_ref, res_ref,
    rhs_ref, dshift_ref, face_ref, col_v, row_v, col_s, row_s, rows_s,
    sb, kt, perm, kb, kf, ya, yb, sq, dg, wv, wa, wb, terms, ta, tb, fadd, onehot_r, onehot_c, img,
    x_s, r_s, d_s, al_s, z_s, inv_s, dsh_s,
    sqf, rsqf, halo, part, rs, ag, back, rback, red,
    load_sem, in_sem, sq_ss, sq_rs, halo_ss, halo_rs, rs_ss, rs_rs, ag_ss, ag_rs, bk_ss, bk_rs, rd_ss, rd_rs,
):
    E = stiff_hbm.shape[0]
    F = face_hbm.shape[1]
    F2 = 2 * F
    J = rhs_hbm.shape[2] // BLOCK
    R = J * n_dom
    H = J // 2
    N = n_slab * n_dom
    slab = lax.axis_index("slab")
    dom = lax.axis_index("dom")
    lin = slab * n_dom + dom
    up = lax.rem(slab + 1, n_slab)
    down = lax.rem(slab + n_slab - 1, n_slab)

    def load_copy(i):
        rows = pl.ds(pl.multiple_of(i * CHUNK, CHUNK), CHUNK)
        return pltpu.make_async_copy(stiff_hbm.at[rows], sb.at[rows], load_sem.at[i])

    in_copies = [
        pltpu.make_async_copy(source, target, in_sem.at[n])
        for n, (source, target) in enumerate((
            (rows_hbm, rows_s), (face_hbm, face_ref), (rhs_hbm, rhs_ref), (dshift_hbm, dshift_ref),
            (col_hbm, col_v), (row_hbm, row_v), (col_hbm, col_s), (row_hbm, row_s),
        ))
    ]
    for i in range(E // CHUNK):
        load_copy(i).start()
        if i == 0:
            for c in in_copies:
                c.start()

    barrier = pltpu.get_barrier_semaphore()

    def greet(k, carry):
        other = lax.rem(lin + k, N)
        pl.semaphore_signal(
            barrier, inc=1, device_id=(other // n_dom, lax.rem(other, n_dom)), device_id_type=MESH
        )
        return carry

    lax.fori_loop(1, N, greet, 0)

    def exchange(src_low, src_up, dst, ss, rs_sem):
        return [
            pltpu.make_async_remote_copy(
                src_ref=src_up, dst_ref=dst.at[0], send_sem=ss.at[0], recv_sem=rs_sem.at[0],
                device_id=(up, dom), device_id_type=MESH,
            ),
            pltpu.make_async_remote_copy(
                src_ref=src_low, dst_ref=dst.at[1], send_sem=ss.at[1], recv_sem=rs_sem.at[1],
                device_id=(down, dom), device_id_type=MESH,
            ),
        ]

    r_s[...] = jnp.zeros(r_s.shape, f32)
    x_s[...] = jnp.zeros(x_s.shape, f32)
    dsh_s[...] = jnp.zeros(dsh_s.shape, f32)
    fadd[...] = jnp.zeros(fadd.shape, f32)
    ya[...] = jnp.zeros(ya.shape, f32)
    yb[...] = jnp.zeros(yb.shape, f32)
    i_out = lax.broadcasted_iota(jnp.int32, perm.shape, 0)
    i_in = lax.broadcasted_iota(jnp.int32, perm.shape, 1)
    perm[...] = jnp.where(i_out == (i_in % ROWS) * GROUP + i_in // ROWS, 1.0, 0.0).astype(bf16)

    for c in in_copies:
        c.wait()
    e_id = lax.broadcasted_iota(jnp.int32, (F2, LANES), 0)
    limit = jnp.where(e_id < F, rows_s[0, 0] - e_id * BLOCK, rows_s[0, 1] - (e_id - F) * BLOCK)

    def aligned(at):
        return at if isinstance(at, int) else pl.multiple_of(at, LANES)

    def sixteen_rows(load, p, acc, store, mask=None, slot=0):
        count = acc.shape[0]
        for half in range(2):
            for quad in range(2):
                start = (p * 4 + half * 2 + quad) * 384
                tiles = [load(aligned(start + t * LANES)).astype(f32) for t in range(3)]
                for k, row in enumerate(rows_of_four(tiles)):
                    if mask is not None:
                        a = p * 16 + half * 8 + quad * 4 + k
                        row = jnp.where(mask > a, row, jnp.zeros_like(row))
                    acc = acc + row * row
                    for g in range(count // 8):
                        kt[slot, pl.ds((g * 2 + half) * 64 + quad * 4 + k, 8, stride=8), :] = row[g * 8 : g * 8 + 8]
        for g in range(count // 8):
            for e in range(8):
                pair = [kt[slot, pl.ds((g * 2 + half) * 64 + e * 8, 8), :] for half in range(2)]
                store(g * 8 + e, jnp.concatenate(pair, axis=0).astype(bf16))
        return acc

    def face_load(start):
        return jnp.concatenate([face_ref[0, :, pl.ds(start, LANES)], face_ref[1, :, pl.ds(start, LANES)]], axis=0)

    def face_step(p, acc):
        def store(e, tile):
            kf[e, pl.ds(pl.multiple_of(p * 16, 16), 16), :] = tile

        return sixteen_rows(lambda start: face_load(start).astype(f32), p, acc, store, limit)

    face_sq = lax.fori_loop(0, BLOCK // 16, face_step, jnp.zeros((F2, LANES), f32))
    sqf[0] = jnp.concatenate([face_sq[:F], jnp.zeros((ROWS - F, LANES), f32)], axis=0)
    sqf[1] = jnp.concatenate([face_sq[F:], jnp.zeros((ROWS - F, LANES), f32)], axis=0)

    pl.semaphore_wait(barrier, N - 1)
    sq_copies = exchange(sqf.at[0], sqf.at[1], rsqf, sq_ss, sq_rs)
    for c in sq_copies:
        c.start()

    for j in range(J):
        for c in range(CASES):
            r_s[j, pl.ds(c, 1), pl.ds(0, BLOCK)] = rhs_ref[c, :, j * BLOCK : (j + 1) * BLOCK]
        dsh_s[pl.ds(j, 1), pl.ds(0, BLOCK)] = dshift_ref[:, j * BLOCK : (j + 1) * BLOCK]

    onehot_r[...] = jnp.where(
        lax.broadcasted_iota(jnp.int32, (R, E), 0) == row_v[...], 1.0, 0.0
    ).astype(bf16)
    onehot_c[...] = jnp.where(
        lax.broadcasted_iota(jnp.int32, (J, E), 0) == col_v[...], 1.0, 0.0
    ).astype(bf16)

    def chunk_step(i, carry):
        load_copy(i).wait()
        base = pl.multiple_of(i * CHUNK, CHUNK)
        sums = [jnp.zeros((CHUNK, LANES), f32) for _ in range(3)]
        for p in range(BLOCK // GROUP):
            rows = []
            for q in range(GROUP // 4):
                start = (p * (GROUP // 4) + q) * 384
                tiles = [sb[pl.ds(base, CHUNK), pl.ds(start + t * LANES, LANES)].astype(f32) for t in range(3)]
                sums = [acc + w * w for acc, w in zip(sums, tiles)]
                rows += rows_of_four(tiles)
            for g in range(CHUNK // ROWS):
                picked = jnp.concatenate([row[g * ROWS : (g + 1) * ROWS] for row in rows], axis=0)
                turned = nn(perm[...], picked.astype(bf16)).astype(bf16)
                kb[pl.ds(base + g * ROWS, ROWS), pl.ds(p * GROUP, GROUP), :] = turned.reshape(ROWS, GROUP, LANES)
        sq[pl.ds(base, CHUNK), :] = sum(rows_of_four(sums))
        return carry

    lax.fori_loop(0, E // CHUNK, chunk_step, 0)

    sq_all = sq[...]
    sq_high = sq_all.astype(bf16)
    sq_low = (sq_all - sq_high.astype(f32)).astype(bf16)
    dg[...] = dsh_s[...] + nn(onehot_c[...], sq_high) + nn(onehot_c[...], sq_low)
    for c in sq_copies:
        c.wait()
    dg[pl.ds(0, F), :] += rsqf[0, pl.ds(0, F), :]
    dg[pl.ds(J - F, F), :] += rsqf[1, pl.ds(0, F), :]
    lane = lax.broadcasted_iota(jnp.int32, (J, LANES), 1)
    inv_s[...] = jnp.where(lane < BLOCK, 1.0 / jnp.where(lane < BLOCK, dg[...], 1.0), 0.0)

    blank = jnp.zeros((2 * ROWS, LANES), bf16)
    case_live = lax.broadcasted_iota(jnp.int32, (ROWS, 1), 0) < CASES
    rz_now = step_size = None

    for it in range(ITERS):
        rz_part = jnp.zeros((ROWS, LANES), f32)
        curv_part = jnp.zeros((ROWS, LANES), f32)
        for j in range(J):
            r_j = r_s[j]
            z_j = inv_s[pl.ds(j, 1), :] * r_j
            z_s[it, j] = z_j
            wv[j] = split(z_j)
            rz_part += r_j * z_j
            curv_part += dsh_s[pl.ds(j, 1), :] * z_j * z_j
        halo_copies = exchange(
            z_s.at[it, pl.ds(0, F)], z_s.at[it, pl.ds(J - F, F)], halo.at[it], halo_ss.at[it], halo_rs.at[it]
        )
        for c in halo_copies:
            c.start()

        for h in range(PARTS):
            rows_h = pl.ds(h * PART, PART)

            def forward_step(s, carry):
                for u in range(UNROLL):
                    e = s * UNROLL + u
                    f = e + E // 2
                    x_e = jnp.concatenate([wv[col_s[0, e]], blank], axis=1)
                    x_f = jnp.concatenate([blank, wv[col_s[0, f]]], axis=1)
                    k_ef = jnp.concatenate([kb[e, rows_h], kb[f, rows_h]], axis=1)
                    y = nt(jnp.concatenate([x_e, x_f], axis=0), k_ef)
                    for n, (flat, where) in enumerate(term_rows(half, s, u) for half in halves(terms)):
                        flat[where, pl.ds(0, PART)] = two(y[n * 2 * ROWS : (n + 1) * 2 * ROWS])
                return carry

            steps(E // 2 // UNROLL, forward_step)
            t = [by_case(terms, c) for c in range(CASES)]
            packed = jnp.concatenate([lay([(x, 0) for x in t[:4]]), lay([(x, 0) for x in t[4:]])], axis=1)
            high = packed.astype(bf16)
            low = (packed - high.astype(f32)).astype(bf16)
            total = nn(onehot_r[...], high) + nn(onehot_r[...], low)
            part[it, h, :, pl.ds(0, J)] = total[:, :LANES].reshape(n_dom, J, LANES)
            rest = total[:, LANES:].reshape(n_dom, 2, H, LANES)
            first, second = (rest[:, half].reshape(n_dom * H, LANES) for half in range(2))
            first = jnp.where(lax.broadcasted_iota(jnp.int32, first.shape, 1) < 2 * PART, first, turn(second, 2 * PART))
            part[it, h, :, pl.ds(J, H)] = first.reshape(n_dom, H, LANES)
            for k in range(1, n_dom):
                other = lax.rem(dom + k, n_dom)
                pltpu.make_async_remote_copy(
                    src_ref=part.at[it, h, other], dst_ref=rs.at[it, h, k - 1],
                    send_sem=rs_ss.at[it, h], recv_sem=rs_rs.at[it, h],
                    device_id=(slab, other), device_id_type=MESH,
                ).start()

        for c in halo_copies:
            c.wait()
        for k in range(2):
            for i in range(F):
                j = k * (J - F) + i
                fadd[j, :, pl.ds(0, BLOCK)] = two(nt(split(halo[it, k, i]), kf[k * F + i]))
        face_parts = []
        for h in range(PARTS):
            t = [fadd.reshape(J * ROWS, LANES)[pl.ds(c, J, stride=ROWS), :] for c in range(CASES)]
            face_parts.append((
                lay([(x, h * PART) for x in t[:4]]),
                lay([(x[half * H : half * H + H], h * PART) for half in range(2) for x in t[4:]]),
            ))

        for h in range(PARTS):
            own = part[it, h, dom] + jnp.concatenate(face_parts[h], axis=0)
            for sem in (rs_ss.at[it, h], rs_rs.at[it, h]):
                wait_bytes(rs.at[it, h], sem)
            for k in range(1, n_dom):
                own = own + rs[it, h, k - 1]
            ag[it, h, dom] = own
            for k in range(1, n_dom):
                other = lax.rem(dom + k, n_dom)
                pltpu.make_async_remote_copy(
                    src_ref=ag.at[it, h, dom], dst_ref=ag.at[it, h, dom],
                    send_sem=ag_ss.at[it, h], recv_sem=ag_rs.at[it, h],
                    device_id=(slab, other), device_id_type=MESH,
                ).start()

        def spread(owner, slot, parts, dst):
            for half in range(2):
                for c in range(CASES):
                    if c < 4:
                        where, start = pl.ds(half * H, H), c * PART
                    else:
                        where, start = pl.ds(J, H), (2 * half + c - 4) * PART
                    tile = lay([(ag[it, h, owner, where], start) for h in parts])
                    dst[slot, pl.ds(half * H * ROWS + c, H, stride=ROWS), :] = tile

        def take_rows(owner, slot, src, dst):
            squares = jnp.zeros((ROWS, LANES), f32)
            for j in range(J):
                y = src[slot, pl.ds(j * ROWS, ROWS), :]
                dst[owner * J + j] = split(y)
                squares += y * y
            return squares

        a_parts, b_parts = tuple(range(PARTS - 1)), (PARTS - 1,)
        spread(dom, 0, a_parts, ya)
        spread(dom, 0, b_parts, yb)
        curv_part += take_rows(dom, 0, ya, wa) + take_rows(dom, 0, yb, wb)
        lane8 = lax.broadcasted_iota(jnp.int32, (ROWS, LANES), 1)
        case8 = lax.broadcasted_iota(jnp.int32, (ROWS, LANES), 0)
        spot = jnp.where(lane8 == case8, jnp.sum(rz_part, axis=1, keepdims=True), 0.0) + jnp.where(
            lane8 == case8 + ROWS, jnp.sum(curv_part, axis=1, keepdims=True), 0.0
        )
        sums = jnp.sum(spot, axis=0, keepdims=True)
        red[it, lin] = sums

        def reduce_copy(k):
            other = lax.rem(lin + k, N)
            return pltpu.make_async_remote_copy(
                src_ref=red.at[it, lin], dst_ref=red.at[it, lin],
                send_sem=rd_ss.at[it], recv_sem=rd_rs.at[it],
                device_id=(other // n_dom, lax.rem(other, n_dom)), device_id_type=MESH,
            )

        def reduce_start(k, carry):
            reduce_copy(k).start()
            return carry

        lax.fori_loop(1, N, reduce_start, 0)
        for k in range(2):
            for i in range(F):
                row = dom * J + (k * (J - F) + i)
                back[it, k, i] = two(
                    nn(wa[row, :, pl.ds(0, BLOCK - PART)], kf[k * F + i, pl.ds(0, BLOCK - PART)])
                    + nn(wb[row, :, pl.ds(0, PART)], kf[k * F + i, pl.ds(BLOCK - PART, PART)])
                )
        back_copies = exchange(back.at[it, 0], back.at[it, 1], rback.at[it], bk_ss.at[it], bk_rs.at[it])
        for c in back_copies:
            c.start()

        for parts, y_buf, w_buf, t_buf in ((a_parts, ya, wa, ta), (b_parts, yb, wb, tb)):
            for h in parts:
                for sem in (ag_ss.at[it, h], ag_rs.at[it, h]):
                    wait_bytes(ag.at[it, h, pl.ds(0, n_dom - 1)], sem)
            for k in range(1, n_dom):
                owner = lax.rem(dom + n_dom - k, n_dom)
                spread(owner, k, parts, y_buf)
                take_rows(owner, k, y_buf, w_buf)
            wide = len(parts) * PART
            rows_p = pl.ds(parts[0] * PART, wide)

            def adjoint_step(s, carry):
                for u in range(UNROLL):
                    e = s * UNROLL + u
                    f = e + E // 2
                    y_e = w_buf[row_s[0, e], :, pl.ds(0, wide)]
                    y_f = w_buf[row_s[0, f], :, pl.ds(0, wide)]
                    k_ef = jnp.concatenate([kb[e, rows_p], kb[f, rows_p]], axis=1)
                    x = nn(jnp.concatenate([y_e, y_f], axis=0), k_ef)
                    for n, (flat, where) in enumerate(term_rows(half, s, u) for half in halves(t_buf)):
                        flat[where, :] = two(x[n * 2 * ROWS : (n + 1) * 2 * ROWS, n * LANES : (n + 1) * LANES])
                return carry

            steps(E // 2 // UNROLL, adjoint_step)
        sel = onehot_c[...]
        img_flat = img.reshape(J * ROWS, LANES)
        for m in range(CASES // 2):
            t = [by_case(ta, c) + by_case(tb, c) for c in (2 * m, 2 * m + 1)]
            t = jnp.concatenate(t, axis=1)
            high = t.astype(bf16)
            low = (t - high.astype(f32)).astype(bf16)
            total = nn(sel, high) + nn(sel, low)
            for k in range(2):
                img_flat[pl.ds(2 * m + k, J, stride=ROWS), :] = total[:, k * LANES : (k + 1) * LANES]
        for c in back_copies:
            c.wait()
        for sem in (rd_ss.at[it], rd_rs.at[it]):
            wait_bytes(red.at[it, pl.ds(0, N - 1)], sem)
        total = jnp.sum(red[it], axis=0)
        rz = jnp.sum(jnp.where(lane8 == case8, total, 0.0), axis=1, keepdims=True)
        curv = jnp.sum(jnp.where(lane8 == case8 + ROWS, total, 0.0), axis=1, keepdims=True)
        if it == 0:
            ratio = None
            step_size = jnp.where(case_live, rz / jnp.where(case_live, curv, 1.0), 0.0)
        else:
            ratio = jnp.where(case_live, rz / jnp.where(case_live, rz_now, 1.0), 0.0)
            bottom = curv - ratio * rz / jnp.where(case_live, step_size, 1.0)
            step_size = jnp.where(case_live, rz / jnp.where(case_live, bottom, 1.0), 0.0)
        rz_now = rz
        row_live = lax.broadcasted_iota(jnp.int32, (ROWS, LANES), 0) < CASES
        for j in range(J):
            z_j = z_s[it, j]
            y = jnp.where(row_live, img[j], 0.0) + dsh_s[pl.ds(j, 1), :] * z_j
            if j < F:
                y = y + rback[it, 0, j]
            if j >= J - F:
                y = y + rback[it, 1, j - (J - F)]
            if it == 0:
                d_j, a_j = z_j, y
            else:
                d_j = z_j + ratio * d_s[j]
                a_j = y + ratio * al_s[j]
            x_j = x_s[j] + step_size * d_j
            r_j = r_s[j] - step_size * a_j
            if it + 1 < ITERS:
                d_s[j] = d_j
                al_s[j] = a_j
            x_s[j] = x_j
            r_s[j] = r_j

    for source, target in ((x_s, sol_ref), (r_s, res_ref)):
        flat_out = jnp.concatenate([source[j, :, pl.ds(0, BLOCK)] for j in range(J)], axis=1)
        for c in range(CASES):
            target[c] = flat_out[c : c + 1]


def solution(mesh):
    n_slab, n_dom = mesh.shape["slab"], mesh.shape["dom"]
    N = n_slab * n_dom

    def body(rhs, dshift, stiff, face_k, elem_col, elem_row, face_rows):
        span = rhs.shape[2]
        J = span // BLOCK
        E = stiff.shape[1]
        F = face_k.shape[2]
        R = J * n_dom
        H = J // 2
        vmem = pl.BlockSpec(memory_space=pltpu.VMEM)
        anywhere = pl.BlockSpec(memory_space=pl.ANY)
        dma = pltpu.SemaphoreType.DMA
        out = pl.pallas_call(
            functools.partial(kernel, n_slab, n_dom),
            out_shape=(
                pltpu.VMEM((CASES, 1, span), f32),
                pltpu.VMEM((CASES, 1, span), f32),
            ),
            in_specs=[anywhere] * 7,
            out_specs=(vmem, vmem),
            scratch_shapes=[
                pltpu.VMEM((CASES, 1, span), f32),
                pltpu.VMEM((1, span), f32),
                pltpu.VMEM((2, F, BLOCK * BLOCK), bf16),
                pltpu.VMEM((1, E), jnp.int32),
                pltpu.VMEM((1, E), jnp.int32),
                pltpu.SMEM((1, E), jnp.int32),
                pltpu.SMEM((1, E), jnp.int32),
                pltpu.SMEM((1, 2), jnp.int32),
                pltpu.VMEM((E, BLOCK * BLOCK), bf16),
                pltpu.VMEM((SLOTS, 2 * F * 16, LANES), f32),
                pltpu.VMEM((ROWS * GROUP, ROWS * GROUP), bf16),
                pltpu.VMEM((E, BLOCK, LANES), bf16),
                pltpu.VMEM((2 * F, BLOCK, LANES), bf16),
                pltpu.VMEM((n_dom, J * ROWS, LANES), f32),
                pltpu.VMEM((n_dom, J * ROWS, LANES), f32),
                pltpu.VMEM((E, LANES), f32),
                pltpu.VMEM((J, LANES), f32),
                pltpu.VMEM((J, 2 * ROWS, LANES), bf16),
                pltpu.VMEM((R, 2 * ROWS, LANES), bf16),
                pltpu.VMEM((R, 2 * ROWS, LANES), bf16),
                pltpu.VMEM((E // ROWS, ROWS, ROWS, LANES), f32),
                pltpu.VMEM((E // ROWS, ROWS, ROWS, LANES), f32),
                pltpu.VMEM((E // ROWS, ROWS, ROWS, LANES), f32),
                pltpu.VMEM((J, ROWS, LANES), f32),
                pltpu.VMEM((R, E), bf16),
                pltpu.VMEM((J, E), bf16),
                pltpu.VMEM((J, ROWS, LANES), f32),
                pltpu.VMEM((J, ROWS, LANES), f32),
                pltpu.VMEM((J, ROWS, LANES), f32),
                pltpu.VMEM((J, ROWS, LANES), f32),
                pltpu.VMEM((J, ROWS, LANES), f32),
                pltpu.VMEM((ITERS, J, ROWS, LANES), f32),
                pltpu.VMEM((J, LANES), f32),
                pltpu.VMEM((J, LANES), f32),
                pltpu.VMEM((2, ROWS, LANES), f32),
                pltpu.VMEM((2, ROWS, LANES), f32),
                pltpu.VMEM((ITERS, 2, F, ROWS, LANES), f32),
                pltpu.VMEM((ITERS, PARTS, n_dom, J + H, LANES), f32),
                pltpu.VMEM((ITERS, PARTS, n_dom - 1, J + H, LANES), f32),
                pltpu.VMEM((ITERS, PARTS, n_dom, J + H, LANES), f32),
                pltpu.VMEM((ITERS, 2, F, ROWS, LANES), f32),
                pltpu.VMEM((ITERS, 2, F, ROWS, LANES), f32),
                pltpu.VMEM((ITERS, N, 1, LANES), f32),
                dma((E // CHUNK,)),
                dma((8,)),
                dma((2,)),
                dma((2,)),
                dma((ITERS, 2)),
                dma((ITERS, 2)),
                dma((ITERS, PARTS)),
                dma((ITERS, PARTS)),
                dma((ITERS, PARTS)),
                dma((ITERS, PARTS)),
                dma((ITERS, 2)),
                dma((ITERS, 2)),
                dma((ITERS,)),
                dma((ITERS,)),
            ],
            compiler_params=pltpu.CompilerParams(
                collective_id=0, has_side_effects=True, vmem_limit_bytes=56 * 1024 * 1024
            ),
        )(
            rhs, dshift, stiff.reshape(E, BLOCK * BLOCK),
            face_k.reshape(2, F, BLOCK * BLOCK), elem_col, elem_row, face_rows,
        )
        return out

    return jax.shard_map(
        body,
        mesh=mesh,
        in_specs=(
            P(None, "slab", "dom"),
            P("slab", "dom"),
            P("slab", "dom", None),
            P("slab", None, "dom", None),
            P("slab", "dom"),
            P("slab", "dom"),
            P("slab", None),
        ),
        out_specs=(P(None, "slab", "dom"), P(None, "slab", "dom")),
        check_vma=False,
    )
```

```python
import functools

import jax
import jax.numpy as jnp
from jax import lax
from jax.experimental import pallas as pl
from jax.experimental.pallas import tpu as pltpu
from jax.sharding import PartitionSpec as P

BLOCK = 96
LANES = 128
CASES = 6
ROWS = 8
ITERS = 2
CHUNK = 128
UNROLL = 128
SLOTS = 1
GROUP = 16
PART = 32
PARTS = BLOCK // PART
MESH = pl.DeviceIdType.MESH
f32 = jnp.float32
bf16 = jnp.bfloat16


def split(x):
    high = x.astype(bf16).astype(f32)
    return jnp.concatenate([high, x - high], axis=0).astype(bf16)


def nn(a, b):
    return lax.dot_general(a, b, (((1,), (0,)), ((), ())), preferred_element_type=f32)


def nt(a, b):
    return lax.dot_general(a, b, (((1,), (1,)), ((), ())), preferred_element_type=f32)


def two(x):
    return x[:ROWS] + x[ROWS:]


def rows_of_four(tiles):
    t0, t1, t2 = tiles
    lane = lax.broadcasted_iota(jnp.int32 if t0.dtype == f32 else jnp.int16, t0.shape, 1)
    return (
        t0,
        turn(jnp.where(lane < 96, t1, t0), 32),
        turn(jnp.where(lane < 64, t2, t1), 64),
        turn(t2, 96),
    )


def turn(x, shift):
    shift %= LANES
    return pltpu.roll(x, shift, 1) if shift else x


def lay(pieces):
    lane = lax.broadcasted_iota(jnp.int32, pieces[0][0].shape, 1)
    out = jnp.zeros_like(pieces[0][0]) if len(pieces) * PART < LANES else None
    for n in reversed(range(len(pieces))):
        tile, start = pieces[n]
        tile = turn(tile, n * PART - start)
        out = tile if out is None else jnp.where(lane < (n + 1) * PART, tile, out)
    return out


def by_case(ref, c):
    return ref[:, c].reshape(ref.shape[0] * ROWS, LANES)


def halves(ref):
    n = ref.shape[0] // 2
    return ref.at[pl.ds(0, n)], ref.at[pl.ds(n, n)]


def term_rows(ref, s, u):
    at = (s * (UNROLL // ROWS) + u // ROWS) * ROWS * ROWS + u % ROWS
    return ref.reshape(ref.shape[0] * ROWS * ROWS, LANES), pl.ds(at, ROWS, stride=ROWS)


def wait_bytes(ref, sem):
    pltpu.make_async_copy(ref, ref, sem).wait()


def steps(count, step):
    if count == 1:
        step(0, 0)
    else:
        lax.fori_loop(0, count, step, 0)


def kernel(
    n_slab, n_dom,
    rhs_hbm, dshift_hbm, stiff_hbm, face_hbm, col_hbm, row_hbm, rows_hbm,
    sol_ref, res_ref,
    rhs_ref, dshift_ref, face_ref, col_v, row_v, col_s, row_s, rows_s,
    sb, kt, perm, kb, kf, ya, sq, dg, wv, wa, terms, ta, fadd, onehot_r, onehot_c, img,
    x_s, r_s, d_s, al_s, z_s, inv_s, dsh_s,
    sqf, rsqf, halo, part, rs, ag, back, rback, red,
    load_sem, in_sem, sq_ss, sq_rs, halo_ss, halo_rs, rs_ss, rs_rs, ag_ss, ag_rs, bk_ss, bk_rs, rd_ss, rd_rs,
):
    E = stiff_hbm.shape[0]
    F = face_hbm.shape[1]
    F2 = 2 * F
    J = rhs_hbm.shape[2] // BLOCK
    R = J * n_dom
    H = J // 2
    N = n_slab * n_dom
    slab = lax.axis_index("slab")
    dom = lax.axis_index("dom")
    lin = slab * n_dom + dom
    up = lax.rem(slab + 1, n_slab)
    down = lax.rem(slab + n_slab - 1, n_slab)

    def load_copy(i):
        rows = pl.ds(pl.multiple_of(i * CHUNK, CHUNK), CHUNK)
        return pltpu.make_async_copy(stiff_hbm.at[rows], sb.at[rows], load_sem.at[i])

    in_copies = [
        pltpu.make_async_copy(source, target, in_sem.at[n])
        for n, (source, target) in enumerate((
            (rows_hbm, rows_s), (face_hbm, face_ref), (rhs_hbm, rhs_ref), (dshift_hbm, dshift_ref),
            (col_hbm, col_v), (row_hbm, row_v), (col_hbm, col_s), (row_hbm, row_s),
        ))
    ]
    for i in range(E // CHUNK):
        load_copy(i).start()
        if i == 0:
            for c in in_copies:
                c.start()

    barrier = pltpu.get_barrier_semaphore()

    def each_other(visit):
        doms = [dom] + [lax.rem(dom + k, n_dom) for k in range(1, n_dom)]
        for other in doms[1:]:
            visit((slab, other))

        def one_slab(k, carry):
            there = lax.rem(slab + k, n_slab)
            for other in doms:
                visit((there, other))
            return carry

        lax.fori_loop(1, n_slab, one_slab, 0)

    each_other(lambda device: pl.semaphore_signal(barrier, inc=1, device_id=device, device_id_type=MESH))

    def exchange(src_low, src_up, dst, ss, rs_sem):
        for n, (src, other) in enumerate(((src_up, up), (src_low, down))):
            pltpu.make_async_remote_copy(
                src_ref=src, dst_ref=dst.at[n], send_sem=ss, recv_sem=rs_sem,
                device_id=(other, dom), device_id_type=MESH,
            ).start()

    def exchanged(dst, ss, rs_sem):
        for sem in (ss, rs_sem):
            wait_bytes(dst, sem)

    r_s[...] = jnp.zeros(r_s.shape, f32)
    x_s[...] = jnp.zeros(x_s.shape, f32)
    dsh_s[...] = jnp.zeros(dsh_s.shape, f32)
    fadd[...] = jnp.zeros(fadd.shape, f32)
    ya[...] = jnp.zeros(ya.shape, f32)
    i_out = lax.broadcasted_iota(jnp.int32, perm.shape, 0)
    i_in = lax.broadcasted_iota(jnp.int32, perm.shape, 1)
    perm[...] = jnp.where(i_out == (i_in % GROUP) * ROWS + i_in // GROUP, 1.0, 0.0).astype(bf16)

    for c in in_copies:
        c.wait()
    e_id = lax.broadcasted_iota(jnp.int32, (F2, LANES), 0)
    limit = jnp.where(e_id < F, rows_s[0, 0] - e_id * BLOCK, rows_s[0, 1] - (e_id - F) * BLOCK)

    def aligned(at):
        return at if isinstance(at, int) else pl.multiple_of(at, LANES)

    def sixteen_rows(load, p, acc, store, mask=None, slot=0):
        count = acc.shape[0]
        for half in range(2):
            for quad in range(2):
                start = (p * 4 + half * 2 + quad) * 384
                tiles = [load(aligned(start + t * LANES)).astype(f32) for t in range(3)]
                for k, row in enumerate(rows_of_four(tiles)):
                    if mask is not None:
                        a = p * 16 + half * 8 + quad * 4 + k
                        row = jnp.where(mask > a, row, jnp.zeros_like(row))
                    acc = acc + row * row
                    for g in range(count // 8):
                        kt[slot, pl.ds((g * 2 + half) * 64 + quad * 4 + k, 8, stride=8), :] = row[g * 8 : g * 8 + 8]
        for g in range(count // 8):
            for e in range(8):
                pair = [kt[slot, pl.ds((g * 2 + half) * 64 + e * 8, 8), :] for half in range(2)]
                store(g * 8 + e, jnp.concatenate(pair, axis=0).astype(bf16))
        return acc

    def face_load(start):
        return jnp.concatenate([face_ref[0, :, pl.ds(start, LANES)], face_ref[1, :, pl.ds(start, LANES)]], axis=0)

    def face_step(p, acc):
        def store(e, tile):
            kf[e, pl.ds(pl.multiple_of(p * 16, 16), 16), :] = tile

        return sixteen_rows(lambda start: face_load(start).astype(f32), p, acc, store, limit)

    face_sq = lax.fori_loop(0, BLOCK // 16, face_step, jnp.zeros((F2, LANES), f32))
    sqf[0] = jnp.concatenate([face_sq[:F], jnp.zeros((ROWS - F, LANES), f32)], axis=0)
    sqf[1] = jnp.concatenate([face_sq[F:], jnp.zeros((ROWS - F, LANES), f32)], axis=0)

    pl.semaphore_wait(barrier, N - 1)
    exchange(sqf.at[0], sqf.at[1], rsqf, sq_ss.at[0], sq_rs.at[0])

    for j in range(J):
        for c in range(CASES):
            r_s[j, pl.ds(c, 1), pl.ds(0, BLOCK)] = rhs_ref[c, :, j * BLOCK : (j + 1) * BLOCK]
        dsh_s[pl.ds(j, 1), pl.ds(0, BLOCK)] = dshift_ref[:, j * BLOCK : (j + 1) * BLOCK]

    onehot_r[...] = jnp.where(
        lax.broadcasted_iota(jnp.int32, (R, E), 0) == row_v[...], 1.0, 0.0
    ).astype(bf16)
    onehot_c[...] = jnp.where(
        lax.broadcasted_iota(jnp.int32, (J, E), 0) == col_v[...], 1.0, 0.0
    ).astype(bf16)

    def chunk_step(i, carry):
        load_copy(i).wait()
        base = pl.multiple_of(i * CHUNK, CHUNK)
        for pair in range(CHUNK // GROUP):
            at = [base + pair * GROUP]
            sums = [[jnp.zeros((GROUP, LANES), f32)] * 3 for _ in at]
            for p in range(BLOCK // GROUP):
                halves_p = []
                for half in range(2):
                    rows = [[]]
                    for q in range(2):
                        start = (p * 4 + half * 2 + q) * 384
                        for n in range(1):
                            tiles = [sb[pl.ds(at[n], GROUP), pl.ds(start + t * LANES, LANES)] for t in range(3)]
                            wide = [t.astype(f32) for t in tiles]
                            sums[n] = [acc + w * w for acc, w in zip(sums[n], wide)]
                            rows[n] += rows_of_four(tiles)
                    picked = jnp.concatenate([jnp.concatenate(r, axis=0) for r in rows], axis=1)
                    halves_p.append(nn(perm[...], picked))
                for n in range(1):
                    both = [x[:, n * LANES : (n + 1) * LANES].reshape(GROUP, ROWS, LANES) for x in halves_p]
                    kb[pl.ds(at[n], GROUP), pl.ds(p * GROUP, GROUP), :] = jnp.concatenate(both, axis=1).astype(bf16)
            for n in range(1):
                sq[pl.ds(at[n], GROUP), :] = sum(rows_of_four(sums[n]))
        return carry

    lax.fori_loop(0, E // CHUNK, chunk_step, 0)

    sq_all = sq[...]
    sq_high = sq_all.astype(bf16)
    sq_low = (sq_all - sq_high.astype(f32)).astype(bf16)
    dg[...] = dsh_s[...] + nn(onehot_c[...], sq_high) + nn(onehot_c[...], sq_low)
    exchanged(rsqf, sq_ss.at[0], sq_rs.at[0])
    dg[pl.ds(0, F), :] += rsqf[0, pl.ds(0, F), :]
    dg[pl.ds(J - F, F), :] += rsqf[1, pl.ds(0, F), :]
    lane = lax.broadcasted_iota(jnp.int32, (J, LANES), 1)
    inv_s[...] = jnp.where(lane < BLOCK, 1.0 / jnp.where(lane < BLOCK, dg[...], 1.0), 0.0)

    blank = jnp.zeros((2 * ROWS, LANES), bf16)
    case_live = lax.broadcasted_iota(jnp.int32, (ROWS, 1), 0) < CASES
    rz_now = step_size = None

    for it in range(ITERS):
        rz_part = jnp.zeros((ROWS, LANES), f32)
        curv_part = jnp.zeros((ROWS, LANES), f32)
        for j in range(J):
            r_j = r_s[j]
            z_j = inv_s[pl.ds(j, 1), :] * r_j
            z_s[it, j] = z_j
            wv[j] = split(z_j)
            rz_part += r_j * z_j
            curv_part += dsh_s[pl.ds(j, 1), :] * z_j * z_j
        exchange(
            z_s.at[it, pl.ds(0, F)], z_s.at[it, pl.ds(J - F, F)], halo.at[it], halo_ss.at[it], halo_rs.at[it]
        )

        for h in range(PARTS):
            rows_h = pl.ds(h * PART, PART)

            def forward_step(s, carry):
                for u in range(UNROLL):
                    e = s * UNROLL + u
                    f = e + E // 2
                    x_e = jnp.concatenate([wv[col_s[0, e]], blank], axis=1)
                    x_f = jnp.concatenate([blank, wv[col_s[0, f]]], axis=1)
                    k_ef = jnp.concatenate([kb[e, rows_h], kb[f, rows_h]], axis=1)
                    y = nt(jnp.concatenate([x_e, x_f], axis=0), k_ef)
                    for n, (flat, where) in enumerate(term_rows(half, s, u) for half in halves(terms)):
                        flat[where, pl.ds(0, PART)] = two(y[n * 2 * ROWS : (n + 1) * 2 * ROWS])
                return carry

            steps(E // 2 // UNROLL, forward_step)
            t = [by_case(terms, c) for c in range(CASES)]
            packed = jnp.concatenate([lay([(x, 0) for x in t[:4]]), lay([(x, 0) for x in t[4:]])], axis=1)
            high = packed.astype(bf16)
            low = (packed - high.astype(f32)).astype(bf16)
            total = nn(onehot_r[...], high) + nn(onehot_r[...], low)
            part[it, h, :, pl.ds(0, J)] = total[:, :LANES].reshape(n_dom, J, LANES)
            rest = total[:, LANES:].reshape(n_dom, 2, H, LANES)
            first, second = (rest[:, half].reshape(n_dom * H, LANES) for half in range(2))
            first = jnp.where(lax.broadcasted_iota(jnp.int32, first.shape, 1) < 2 * PART, first, turn(second, 2 * PART))
            part[it, h, :, pl.ds(J, H)] = first.reshape(n_dom, H, LANES)
            for k in range(1, n_dom):
                other = lax.rem(dom + k, n_dom)
                pltpu.make_async_remote_copy(
                    src_ref=part.at[it, h, other], dst_ref=rs.at[it, h, k - 1],
                    send_sem=rs_ss.at[it, h], recv_sem=rs_rs.at[it, h],
                    device_id=(slab, other), device_id_type=MESH,
                ).start()

        exchanged(halo.at[it], halo_ss.at[it], halo_rs.at[it])
        for k in range(2):
            for i in range(F):
                j = k * (J - F) + i
                fadd[j, :, pl.ds(0, BLOCK)] = two(nt(split(halo[it, k, i]), kf[k * F + i]))
        face_parts = []
        for h in range(PARTS):
            t = [fadd.reshape(J * ROWS, LANES)[pl.ds(c, J, stride=ROWS), :] for c in range(CASES)]
            face_parts.append((
                lay([(x, h * PART) for x in t[:4]]),
                lay([(x[half * H : half * H + H], h * PART) for half in range(2) for x in t[4:]]),
            ))

        for h in range(PARTS):
            own = part[it, h, dom] + jnp.concatenate(face_parts[h], axis=0)
            for sem in (rs_ss.at[it, h], rs_rs.at[it, h]):
                wait_bytes(rs.at[it, h], sem)
            for k in range(1, n_dom):
                own = own + rs[it, h, k - 1]
            ag[it, h, dom] = own
            for k in range(1, n_dom):
                other = lax.rem(dom + k, n_dom)
                pltpu.make_async_remote_copy(
                    src_ref=ag.at[it, h, dom], dst_ref=ag.at[it, h, dom],
                    send_sem=ag_ss.at[it, h], recv_sem=ag_rs.at[it, h],
                    device_id=(slab, other), device_id_type=MESH,
                ).start()

        def spread(owner, slot, parts, dst):
            for half in range(2):
                for c in range(CASES):
                    if c < 4:
                        where, start = pl.ds(half * H, H), c * PART
                    else:
                        where, start = pl.ds(J, H), (2 * half + c - 4) * PART
                    tile = lay([(ag[it, h, owner, where], start) for h in parts])
                    dst[slot, pl.ds(half * H * ROWS + c, H, stride=ROWS), :] = tile

        def take_rows(owner, slot, src, dst):
            squares = jnp.zeros((ROWS, LANES), f32)
            for j in range(J):
                y = src[slot, pl.ds(j * ROWS, ROWS), :]
                dst[owner * J + j] = split(y)
                squares += y * y
            return squares

        for h in range(PARTS):
            spread(dom, 0, (h,), ya.at[h])
            curv_part += take_rows(dom, 0, ya.at[h], wa.at[h])
        lane8 = lax.broadcasted_iota(jnp.int32, (ROWS, LANES), 1)
        case8 = lax.broadcasted_iota(jnp.int32, (ROWS, LANES), 0)
        spot = jnp.where(lane8 == case8, jnp.sum(rz_part, axis=1, keepdims=True), 0.0) + jnp.where(
            lane8 == case8 + ROWS, jnp.sum(curv_part, axis=1, keepdims=True), 0.0
        )
        sums = jnp.sum(spot, axis=0, keepdims=True)
        red[it, lin] = sums

        each_other(
            lambda device: pltpu.make_async_remote_copy(
                src_ref=red.at[it, lin], dst_ref=red.at[it, lin], send_sem=rd_ss.at[it], recv_sem=rd_rs.at[it],
                device_id=device, device_id_type=MESH,
            ).start()
        )
        for k in range(2):
            for i in range(F):
                row = dom * J + (k * (J - F) + i)
                back[it, k, i] = two(sum(
                    nn(wa[h, row, :, pl.ds(0, PART)], kf[k * F + i, pl.ds(h * PART, PART)]) for h in range(PARTS)
                ))
        exchange(back.at[it, 0], back.at[it, 1], rback.at[it], bk_ss.at[it], bk_rs.at[it])

        for parts, y_buf, w_buf, t_buf in [((h,), ya.at[h], wa.at[h], ta.at[h]) for h in range(PARTS)]:
            for h in parts:
                for sem in (ag_ss.at[it, h], ag_rs.at[it, h]):
                    wait_bytes(ag.at[it, h, pl.ds(0, n_dom - 1)], sem)
            for k in range(1, n_dom):
                owner = lax.rem(dom + n_dom - k, n_dom)
                spread(owner, k, parts, y_buf)
                take_rows(owner, k, y_buf, w_buf)
            wide = len(parts) * PART
            rows_p = pl.ds(parts[0] * PART, wide)

            def adjoint_step(s, carry):
                for u in range(UNROLL):
                    e = s * UNROLL + u
                    f = e + E // 2
                    y_e = w_buf[row_s[0, e], :, pl.ds(0, wide)]
                    y_f = w_buf[row_s[0, f], :, pl.ds(0, wide)]
                    k_ef = jnp.concatenate([kb[e, rows_p], kb[f, rows_p]], axis=1)
                    x = nn(jnp.concatenate([y_e, y_f], axis=0), k_ef)
                    for n, (flat, where) in enumerate(term_rows(half, s, u) for half in halves(t_buf)):
                        flat[where, :] = two(x[n * 2 * ROWS : (n + 1) * 2 * ROWS, n * LANES : (n + 1) * LANES])
                return carry

            steps(E // 2 // UNROLL, adjoint_step)
        sel = onehot_c[...]
        img_flat = img.reshape(J * ROWS, LANES)
        for m in range(CASES // 2):
            t = [sum(by_case(ta.at[h], c) for h in range(PARTS)) for c in (2 * m, 2 * m + 1)]
            t = jnp.concatenate(t, axis=1)
            high = t.astype(bf16)
            low = (t - high.astype(f32)).astype(bf16)
            total = nn(sel, high) + nn(sel, low)
            for k in range(2):
                img_flat[pl.ds(2 * m + k, J, stride=ROWS), :] = total[:, k * LANES : (k + 1) * LANES]
        exchanged(rback.at[it], bk_ss.at[it], bk_rs.at[it])
        for sem in (rd_ss.at[it], rd_rs.at[it]):
            wait_bytes(red.at[it, pl.ds(0, N - 1)], sem)
        total = jnp.sum(red[it], axis=0)
        rz = jnp.sum(jnp.where(lane8 == case8, total, 0.0), axis=1, keepdims=True)
        curv = jnp.sum(jnp.where(lane8 == case8 + ROWS, total, 0.0), axis=1, keepdims=True)
        if it == 0:
            ratio = None
            step_size = jnp.where(case_live, rz / jnp.where(case_live, curv, 1.0), 0.0)
        else:
            ratio = jnp.where(case_live, rz / jnp.where(case_live, rz_now, 1.0), 0.0)
            bottom = curv - ratio * rz / jnp.where(case_live, step_size, 1.0)
            step_size = jnp.where(case_live, rz / jnp.where(case_live, bottom, 1.0), 0.0)
        rz_now = rz
        row_live = lax.broadcasted_iota(jnp.int32, (ROWS, LANES), 0) < CASES
        for j in range(J):
            z_j = z_s[it, j]
            y = jnp.where(row_live, img[j], 0.0) + dsh_s[pl.ds(j, 1), :] * z_j
            if j < F:
                y = y + rback[it, 0, j]
            if j >= J - F:
                y = y + rback[it, 1, j - (J - F)]
            if it == 0:
                d_j, a_j = z_j, y
            else:
                d_j = z_j + ratio * d_s[j]
                a_j = y + ratio * al_s[j]
            x_j = x_s[j] + step_size * d_j
            r_j = r_s[j] - step_size * a_j
            if it + 1 < ITERS:
                d_s[j] = d_j
                al_s[j] = a_j
            x_s[j] = x_j
            r_s[j] = r_j

    for source, target in ((x_s, sol_ref), (r_s, res_ref)):
        flat_out = jnp.concatenate([source[j, :, pl.ds(0, BLOCK)] for j in range(J)], axis=1)
        for c in range(CASES):
            target[c] = flat_out[c : c + 1]


def solution(mesh):
    n_slab, n_dom = mesh.shape["slab"], mesh.shape["dom"]
    N = n_slab * n_dom

    def body(rhs, dshift, stiff, face_k, elem_col, elem_row, face_rows):
        span = rhs.shape[2]
        J = span // BLOCK
        E = stiff.shape[1]
        F = face_k.shape[2]
        R = J * n_dom
        H = J // 2
        vmem = pl.BlockSpec(memory_space=pltpu.VMEM)
        anywhere = pl.BlockSpec(memory_space=pl.ANY)
        dma = pltpu.SemaphoreType.DMA
        out = pl.pallas_call(
            functools.partial(kernel, n_slab, n_dom),
            out_shape=(
                pltpu.VMEM((CASES, 1, span), f32),
                pltpu.VMEM((CASES, 1, span), f32),
            ),
            in_specs=[anywhere] * 7,
            out_specs=(vmem, vmem),
            scratch_shapes=[
                pltpu.VMEM((CASES, 1, span), f32),
                pltpu.VMEM((1, span), f32),
                pltpu.VMEM((2, F, BLOCK * BLOCK), bf16),
                pltpu.VMEM((1, E), jnp.int32),
                pltpu.VMEM((1, E), jnp.int32),
                pltpu.SMEM((1, E), jnp.int32),
                pltpu.SMEM((1, E), jnp.int32),
                pltpu.SMEM((1, 2), jnp.int32),
                pltpu.VMEM((E, BLOCK * BLOCK), bf16),
                pltpu.VMEM((SLOTS, 2 * F * 16, LANES), f32),
                pltpu.VMEM((ROWS * GROUP, ROWS * GROUP), bf16),
                pltpu.VMEM((E, BLOCK, LANES), bf16),
                pltpu.VMEM((2 * F, BLOCK, LANES), bf16),
                pltpu.VMEM((PARTS, n_dom, J * ROWS, LANES), f32),
                pltpu.VMEM((E, LANES), f32),
                pltpu.VMEM((J, LANES), f32),
                pltpu.VMEM((J, 2 * ROWS, LANES), bf16),
                pltpu.VMEM((PARTS, R, 2 * ROWS, LANES), bf16),
                pltpu.VMEM((E // ROWS, ROWS, ROWS, LANES), f32),
                pltpu.VMEM((PARTS, E // ROWS, ROWS, ROWS, LANES), f32),
                pltpu.VMEM((J, ROWS, LANES), f32),
                pltpu.VMEM((R, E), bf16),
                pltpu.VMEM((J, E), bf16),
                pltpu.VMEM((J, ROWS, LANES), f32),
                pltpu.VMEM((J, ROWS, LANES), f32),
                pltpu.VMEM((J, ROWS, LANES), f32),
                pltpu.VMEM((J, ROWS, LANES), f32),
                pltpu.VMEM((J, ROWS, LANES), f32),
                pltpu.VMEM((ITERS, J, ROWS, LANES), f32),
                pltpu.VMEM((J, LANES), f32),
                pltpu.VMEM((J, LANES), f32),
                pltpu.VMEM((2, ROWS, LANES), f32),
                pltpu.VMEM((2, ROWS, LANES), f32),
                pltpu.VMEM((ITERS, 2, F, ROWS, LANES), f32),
                pltpu.VMEM((ITERS, PARTS, n_dom, J + H, LANES), f32),
                pltpu.VMEM((ITERS, PARTS, n_dom - 1, J + H, LANES), f32),
                pltpu.VMEM((ITERS, PARTS, n_dom, J + H, LANES), f32),
                pltpu.VMEM((ITERS, 2, F, ROWS, LANES), f32),
                pltpu.VMEM((ITERS, 2, F, ROWS, LANES), f32),
                pltpu.VMEM((ITERS, N, 1, LANES), f32),
                dma((E // CHUNK,)),
                dma((8,)),
                dma((1,)),
                dma((1,)),
                dma((ITERS,)),
                dma((ITERS,)),
                dma((ITERS, PARTS)),
                dma((ITERS, PARTS)),
                dma((ITERS, PARTS)),
                dma((ITERS, PARTS)),
                dma((ITERS,)),
                dma((ITERS,)),
                dma((ITERS,)),
                dma((ITERS,)),
            ],
            compiler_params=pltpu.CompilerParams(
                collective_id=0, has_side_effects=True, vmem_limit_bytes=56 * 1024 * 1024
            ),
        )(
            rhs, dshift, stiff.reshape(E, BLOCK * BLOCK),
            face_k.reshape(2, F, BLOCK * BLOCK), elem_col, elem_row, face_rows,
        )
        return out

    return jax.shard_map(
        body,
        mesh=mesh,
        in_specs=(
            P(None, "slab", "dom"),
            P("slab", "dom"),
            P("slab", "dom", None),
            P("slab", None, "dom", None),
            P("slab", "dom"),
            P("slab", "dom"),
            P("slab", None),
        ),
        out_specs=(P(None, "slab", "dom"), P(None, "slab", "dom")),
        check_vma=False,
    )
```

```python
import functools

import jax
import jax.numpy as jnp
from jax import lax
from jax.experimental import pallas as pl
from jax.experimental.pallas import tpu as pltpu
from jax.sharding import PartitionSpec as P

BLOCK = 96
LANES = 128
CASES = 6
ROWS = 8
ITERS = 2
CHUNK = 128
UNROLL = 128
SLOTS = 1
GROUP = 16
PART = 32
PARTS = BLOCK // PART
MESH = pl.DeviceIdType.MESH
f32 = jnp.float32
bf16 = jnp.bfloat16


def split(x):
    high = x.astype(bf16).astype(f32)
    return jnp.concatenate([high, x - high], axis=0).astype(bf16)


def nn(a, b):
    return lax.dot_general(a, b, (((1,), (0,)), ((), ())), preferred_element_type=f32)


def nt(a, b):
    return lax.dot_general(a, b, (((1,), (1,)), ((), ())), preferred_element_type=f32)


def two(x):
    return x[:ROWS] + x[ROWS:]


def rows_of_four(tiles):
    t0, t1, t2 = tiles
    lane = lax.broadcasted_iota(jnp.int32 if t0.dtype == f32 else jnp.int16, t0.shape, 1)
    return (
        t0,
        turn(jnp.where(lane < 96, t1, t0), 32),
        turn(jnp.where(lane < 64, t2, t1), 64),
        turn(t2, 96),
    )


def turn(x, shift):
    shift %= LANES
    return pltpu.roll(x, shift, 1) if shift else x


def lay(pieces):
    lane = lax.broadcasted_iota(jnp.int32, pieces[0][0].shape, 1)
    out = jnp.zeros_like(pieces[0][0]) if len(pieces) * PART < LANES else None
    for n in reversed(range(len(pieces))):
        tile, start = pieces[n]
        tile = turn(tile, n * PART - start)
        out = tile if out is None else jnp.where(lane < (n + 1) * PART, tile, out)
    return out


def by_case(ref, c):
    return ref[:, c].reshape(ref.shape[0] * ROWS, LANES)


def halves(ref):
    n = ref.shape[0] // 2
    return ref.at[pl.ds(0, n)], ref.at[pl.ds(n, n)]


def term_rows(ref, s, u):
    at = (s * (UNROLL // ROWS) + u // ROWS) * ROWS * ROWS + u % ROWS
    return ref.reshape(ref.shape[0] * ROWS * ROWS, LANES), pl.ds(at, ROWS, stride=ROWS)


def wait_bytes(ref, sem):
    pltpu.make_async_copy(ref, ref, sem).wait()


def steps(count, step):
    if count == 1:
        step(0, 0)
    else:
        lax.fori_loop(0, count, step, 0)


def kernel(
    n_slab, n_dom,
    rhs_hbm, dshift_hbm, stiff_hbm, face_hbm, col_hbm, row_hbm, rows_hbm,
    sol_ref, res_ref,
    rhs_ref, dshift_ref, face_ref, col_v, row_v, col_s, row_s, rows_s,
    sb, kt, perm, kb, kf, ya, sq, dg, wv, wa, terms, ta, fadd, onehot_r, onehot_c, img,
    x_s, r_s, d_s, al_s, z_s, inv_s, dsh_s,
    sqf, rsqf, halo, part, rs, ag, back, rback, red,
    load_sem, in_sem, sq_ss, sq_rs, halo_ss, halo_rs, rs_ss, rs_rs, ag_ss, ag_rs, bk_ss, bk_rs, rd_ss, rd_rs,
):
    E = stiff_hbm.shape[0]
    F = face_hbm.shape[1]
    F2 = 2 * F
    J = rhs_hbm.shape[2] // BLOCK
    R = J * n_dom
    H = J // 2
    N = n_slab * n_dom
    slab = lax.axis_index("slab")
    dom = lax.axis_index("dom")
    lin = slab * n_dom + dom
    up = lax.rem(slab + 1, n_slab)
    down = lax.rem(slab + n_slab - 1, n_slab)

    def load_copy(i):
        rows = pl.ds(pl.multiple_of(i * CHUNK, CHUNK), CHUNK)
        return pltpu.make_async_copy(stiff_hbm.at[rows], sb.at[rows], load_sem.at[i])

    in_copies = [
        pltpu.make_async_copy(source, target, in_sem.at[n])
        for n, (source, target) in enumerate((
            (rows_hbm, rows_s), (face_hbm, face_ref), (rhs_hbm, rhs_ref), (dshift_hbm, dshift_ref),
            (col_hbm, col_v), (row_hbm, row_v), (col_hbm, col_s), (row_hbm, row_s),
        ))
    ]
    for i in range(E // CHUNK):
        load_copy(i).start()
        if i == 0:
            for c in in_copies:
                c.start()

    barrier = pltpu.get_barrier_semaphore()

    def each_other(visit):
        doms = [dom] + [lax.rem(dom + k, n_dom) for k in range(1, n_dom)]
        for other in doms[1:]:
            visit((slab, other))

        def one_slab(k, carry):
            there = lax.rem(slab + k, n_slab)
            for other in doms:
                visit((there, other))
            return carry

        lax.fori_loop(1, n_slab, one_slab, 0)

    each_other(lambda device: pl.semaphore_signal(barrier, inc=1, device_id=device, device_id_type=MESH))

    def exchange(src_low, src_up, dst, ss, rs_sem):
        for n, (src, other) in enumerate(((src_up, up), (src_low, down))):
            pltpu.make_async_remote_copy(
                src_ref=src, dst_ref=dst.at[n], send_sem=ss, recv_sem=rs_sem,
                device_id=(other, dom), device_id_type=MESH,
            ).start()

    def exchanged(dst, ss, rs_sem):
        for sem in (ss, rs_sem):
            wait_bytes(dst, sem)

    r_s[...] = jnp.zeros(r_s.shape, f32)
    x_s[...] = jnp.zeros(x_s.shape, f32)
    dsh_s[...] = jnp.zeros(dsh_s.shape, f32)
    fadd[...] = jnp.zeros(fadd.shape, f32)
    ya[...] = jnp.zeros(ya.shape, f32)
    i_out = lax.broadcasted_iota(jnp.int32, perm.shape, 0)
    i_in = lax.broadcasted_iota(jnp.int32, perm.shape, 1)
    perm[...] = jnp.where(i_out == (i_in % GROUP) * ROWS + i_in // GROUP, 1.0, 0.0).astype(bf16)

    for c in in_copies:
        c.wait()
    e_id = lax.broadcasted_iota(jnp.int32, (F2, LANES), 0)
    limit = jnp.where(e_id < F, rows_s[0, 0] - e_id * BLOCK, rows_s[0, 1] - (e_id - F) * BLOCK)

    def aligned(at):
        return at if isinstance(at, int) else pl.multiple_of(at, LANES)

    def sixteen_rows(load, p, acc, store, mask=None, slot=0):
        count = acc.shape[0]
        for half in range(2):
            for quad in range(2):
                start = (p * 4 + half * 2 + quad) * 384
                tiles = [load(aligned(start + t * LANES)).astype(f32) for t in range(3)]
                for k, row in enumerate(rows_of_four(tiles)):
                    if mask is not None:
                        a = p * 16 + half * 8 + quad * 4 + k
                        row = jnp.where(mask > a, row, jnp.zeros_like(row))
                    acc = acc + row * row
                    for g in range(count // 8):
                        kt[slot, pl.ds((g * 2 + half) * 64 + quad * 4 + k, 8, stride=8), :] = row[g * 8 : g * 8 + 8]
        for g in range(count // 8):
            for e in range(8):
                pair = [kt[slot, pl.ds((g * 2 + half) * 64 + e * 8, 8), :] for half in range(2)]
                store(g * 8 + e, jnp.concatenate(pair, axis=0).astype(bf16))
        return acc

    def face_load(start):
        return jnp.concatenate([face_ref[0, :, pl.ds(start, LANES)], face_ref[1, :, pl.ds(start, LANES)]], axis=0)

    def face_step(p, acc):
        def store(e, tile):
            kf[e, pl.ds(pl.multiple_of(p * 16, 16), 16), :] = tile

        return sixteen_rows(lambda start: face_load(start).astype(f32), p, acc, store, limit)

    face_sq = lax.fori_loop(0, BLOCK // 16, face_step, jnp.zeros((F2, LANES), f32))
    sqf[0] = jnp.concatenate([face_sq[:F], jnp.zeros((ROWS - F, LANES), f32)], axis=0)
    sqf[1] = jnp.concatenate([face_sq[F:], jnp.zeros((ROWS - F, LANES), f32)], axis=0)

    pl.semaphore_wait(barrier, N - 1)
    exchange(sqf.at[0], sqf.at[1], rsqf, sq_ss.at[0], sq_rs.at[0])

    for j in range(J):
        for c in range(CASES):
            r_s[j, pl.ds(c, 1), pl.ds(0, BLOCK)] = rhs_ref[c, :, j * BLOCK : (j + 1) * BLOCK]
        dsh_s[pl.ds(j, 1), pl.ds(0, BLOCK)] = dshift_ref[:, j * BLOCK : (j + 1) * BLOCK]

    onehot_r[...] = jnp.where(
        lax.broadcasted_iota(jnp.int32, (R, E), 0) == row_v[...], 1.0, 0.0
    ).astype(bf16)
    onehot_c[...] = jnp.where(
        lax.broadcasted_iota(jnp.int32, (J, E), 0) == col_v[...], 1.0, 0.0
    ).astype(bf16)

    def chunk_step(i, carry):
        load_copy(i).wait()
        base = pl.multiple_of(i * CHUNK, CHUNK)
        for pair in range(CHUNK // GROUP):
            at = [base + pair * GROUP]
            sums = [[jnp.zeros((GROUP, LANES), f32)] * 3 for _ in at]
            for p in range(BLOCK // GROUP):
                halves_p = []
                for half in range(2):
                    rows = [[]]
                    for q in range(2):
                        start = (p * 4 + half * 2 + q) * 384
                        for n in range(1):
                            tiles = [sb[pl.ds(at[n], GROUP), pl.ds(start + t * LANES, LANES)] for t in range(3)]
                            wide = [t.astype(f32) for t in tiles]
                            sums[n] = [acc + w * w for acc, w in zip(sums[n], wide)]
                            rows[n] += rows_of_four(tiles)
                    picked = jnp.concatenate([jnp.concatenate(r, axis=0) for r in rows], axis=1)
                    halves_p.append(nn(perm[...], picked))
                for n in range(1):
                    both = [x[:, n * LANES : (n + 1) * LANES].reshape(GROUP, ROWS, LANES) for x in halves_p]
                    kb[pl.ds(at[n], GROUP), pl.ds(p * GROUP, GROUP), :] = jnp.concatenate(both, axis=1).astype(bf16)
            for n in range(1):
                sq[pl.ds(at[n], GROUP), :] = sum(rows_of_four(sums[n]))
        return carry

    lax.fori_loop(0, E // CHUNK, chunk_step, 0)

    sq_all = sq[...]
    sq_high = sq_all.astype(bf16)
    sq_low = (sq_all - sq_high.astype(f32)).astype(bf16)
    dg[...] = dsh_s[...] + nn(onehot_c[...], sq_high) + nn(onehot_c[...], sq_low)
    exchanged(rsqf, sq_ss.at[0], sq_rs.at[0])
    dg[pl.ds(0, F), :] += rsqf[0, pl.ds(0, F), :]
    dg[pl.ds(J - F, F), :] += rsqf[1, pl.ds(0, F), :]
    lane = lax.broadcasted_iota(jnp.int32, (J, LANES), 1)
    inv_s[...] = jnp.where(lane < BLOCK, 1.0 / jnp.where(lane < BLOCK, dg[...], 1.0), 0.0)

    blank = jnp.zeros((2 * ROWS, LANES), bf16)
    case_live = lax.broadcasted_iota(jnp.int32, (ROWS, 1), 0) < CASES
    rz_now = step_size = None

    for it in range(ITERS):
        rz_part = jnp.zeros((ROWS, LANES), f32)
        curv_part = jnp.zeros((ROWS, LANES), f32)
        for j in range(J):
            r_j = r_s[j]
            z_j = inv_s[pl.ds(j, 1), :] * r_j
            z_s[it, j] = z_j
            wv[j] = split(z_j)
            rz_part += r_j * z_j
            curv_part += dsh_s[pl.ds(j, 1), :] * z_j * z_j
        exchange(
            z_s.at[it, pl.ds(0, F)], z_s.at[it, pl.ds(J - F, F)], halo.at[it], halo_ss.at[it], halo_rs.at[it]
        )

        for h in range(PARTS):
            rows_h = pl.ds(h * PART, PART)

            def forward_step(s, carry):
                for u in range(UNROLL):
                    e = s * UNROLL + u
                    f = e + E // 2
                    x_e = jnp.concatenate([wv[col_s[0, e]], blank], axis=1)
                    x_f = jnp.concatenate([blank, wv[col_s[0, f]]], axis=1)
                    k_ef = jnp.concatenate([kb[e, rows_h], kb[f, rows_h]], axis=1)
                    y = nt(jnp.concatenate([x_e, x_f], axis=0), k_ef)
                    for n, (flat, where) in enumerate(term_rows(half, s, u) for half in halves(terms)):
                        flat[where, pl.ds(0, PART)] = two(y[n * 2 * ROWS : (n + 1) * 2 * ROWS])
                return carry

            steps(E // 2 // UNROLL, forward_step)
            t = [by_case(terms, c) for c in range(CASES)]
            packed = jnp.concatenate([lay([(x, 0) for x in t[:4]]), lay([(x, 0) for x in t[4:]])], axis=1)
            high = packed.astype(bf16)
            low = (packed - high.astype(f32)).astype(bf16)
            total = nn(onehot_r[...], high) + nn(onehot_r[...], low)
            part[it, h, :, pl.ds(0, J)] = total[:, :LANES].reshape(n_dom, J, LANES)
            rest = total[:, LANES:].reshape(n_dom, 2, H, LANES)
            first, second = (rest[:, half].reshape(n_dom * H, LANES) for half in range(2))
            first = jnp.where(lax.broadcasted_iota(jnp.int32, first.shape, 1) < 2 * PART, first, turn(second, 2 * PART))
            part[it, h, :, pl.ds(J, H)] = first.reshape(n_dom, H, LANES)
            for k in range(1, n_dom):
                other = lax.rem(dom + k, n_dom)
                pltpu.make_async_remote_copy(
                    src_ref=part.at[it, h, other], dst_ref=rs.at[it, h, k - 1],
                    send_sem=rs_ss.at[it, h], recv_sem=rs_rs.at[it, h],
                    device_id=(slab, other), device_id_type=MESH,
                ).start()

        exchanged(halo.at[it], halo_ss.at[it], halo_rs.at[it])
        for k in range(2):
            for i in range(F):
                j = k * (J - F) + i
                fadd[j, :, pl.ds(0, BLOCK)] = two(nt(split(halo[it, k, i]), kf[k * F + i]))
        face_parts = []
        for h in range(PARTS):
            t = [fadd.reshape(J * ROWS, LANES)[pl.ds(c, J, stride=ROWS), :] for c in range(CASES)]
            face_parts.append((
                lay([(x, h * PART) for x in t[:4]]),
                lay([(x[half * H : half * H + H], h * PART) for half in range(2) for x in t[4:]]),
            ))

        for h in range(PARTS):
            own = part[it, h, dom] + jnp.concatenate(face_parts[h], axis=0)
            for sem in (rs_ss.at[it, h], rs_rs.at[it, h]):
                wait_bytes(rs.at[it, h], sem)
            for k in range(1, n_dom):
                own = own + rs[it, h, k - 1]
            ag[it, h, dom] = own
            for k in range(1, n_dom):
                other = lax.rem(dom + k, n_dom)
                pltpu.make_async_remote_copy(
                    src_ref=ag.at[it, h, dom], dst_ref=ag.at[it, h, dom],
                    send_sem=ag_ss.at[it, h], recv_sem=ag_rs.at[it, h],
                    device_id=(slab, other), device_id_type=MESH,
                ).start()

        def spread(owner, slot, parts, dst):
            for half in range(2):
                for c in range(CASES):
                    if c < 4:
                        where, start = pl.ds(half * H, H), c * PART
                    else:
                        where, start = pl.ds(J, H), (2 * half + c - 4) * PART
                    tile = lay([(ag[it, h, owner, where], start) for h in parts])
                    dst[slot, pl.ds(half * H * ROWS + c, H, stride=ROWS), :] = tile

        def take_rows(owner, slot, src, dst):
            squares = jnp.zeros((ROWS, LANES), f32)
            for j in range(J):
                y = src[slot, pl.ds(j * ROWS, ROWS), :]
                dst[owner * J + j] = split(y)
                squares += y * y
            return squares

        for h in range(PARTS):
            spread(dom, 0, (h,), ya.at[h])
            curv_part += take_rows(dom, 0, ya.at[h], wa.at[h])
        lane8 = lax.broadcasted_iota(jnp.int32, (ROWS, LANES), 1)
        case8 = lax.broadcasted_iota(jnp.int32, (ROWS, LANES), 0)
        spot = jnp.where(lane8 == case8, jnp.sum(rz_part, axis=1, keepdims=True), 0.0) + jnp.where(
            lane8 == case8 + ROWS, jnp.sum(curv_part, axis=1, keepdims=True), 0.0
        )
        sums = jnp.sum(spot, axis=0, keepdims=True)
        red[it, lin] = sums

        each_other(
            lambda device: pltpu.make_async_remote_copy(
                src_ref=red.at[it, lin], dst_ref=red.at[it, lin], send_sem=rd_ss.at[it], recv_sem=rd_rs.at[it],
                device_id=device, device_id_type=MESH,
            ).start()
        )
        for k in range(2):
            for i in range(F):
                row = dom * J + (k * (J - F) + i)
                back[it, k, i] = two(sum(
                    nn(wa[h, row, :, pl.ds(0, PART)], kf[k * F + i, pl.ds(h * PART, PART)]) for h in range(PARTS)
                ))
        exchange(back.at[it, 0], back.at[it, 1], rback.at[it], bk_ss.at[it], bk_rs.at[it])

        for parts, y_buf, w_buf, t_buf in [((h,), ya.at[h], wa.at[h], ta.at[h]) for h in range(PARTS)]:
            for h in parts:
                for sem in (ag_ss.at[it, h], ag_rs.at[it, h]):
                    wait_bytes(ag.at[it, h, pl.ds(0, n_dom - 1)], sem)
            for k in range(1, n_dom):
                owner = lax.rem(dom + n_dom - k, n_dom)
                spread(owner, k, parts, y_buf)
                take_rows(owner, k, y_buf, w_buf)
            wide = len(parts) * PART
            rows_p = pl.ds(parts[0] * PART, wide)

            def adjoint_step(s, carry):
                for u in range(UNROLL):
                    e = s * UNROLL + u
                    f = e + E // 2
                    y_e = w_buf[row_s[0, e], :, pl.ds(0, wide)]
                    y_f = w_buf[row_s[0, f], :, pl.ds(0, wide)]
                    k_ef = jnp.concatenate([kb[e, rows_p], kb[f, rows_p]], axis=1)
                    x = nn(jnp.concatenate([y_e, y_f], axis=0), k_ef)
                    for n, (flat, where) in enumerate(term_rows(half, s, u) for half in halves(t_buf)):
                        flat[where, :] = two(x[n * 2 * ROWS : (n + 1) * 2 * ROWS, n * LANES : (n + 1) * LANES])
                return carry

            steps(E // 2 // UNROLL, adjoint_step)
        sel = onehot_c[...]
        img_flat = img.reshape(J * ROWS, LANES)
        for m in range(CASES // 2):
            t = [sum(by_case(ta.at[h], c) for h in range(PARTS)) for c in (2 * m, 2 * m + 1)]
            t = jnp.concatenate(t, axis=1)
            high = t.astype(bf16)
            low = (t - high.astype(f32)).astype(bf16)
            total = nn(sel, high) + nn(sel, low)
            for k in range(2):
                img_flat[pl.ds(2 * m + k, J, stride=ROWS), :] = total[:, k * LANES : (k + 1) * LANES]
        exchanged(rback.at[it], bk_ss.at[it], bk_rs.at[it])
        for sem in (rd_ss.at[it], rd_rs.at[it]):
            wait_bytes(red.at[it, pl.ds(0, N - 1)], sem)
        total = jnp.sum(red[it], axis=0)
        rz = jnp.sum(jnp.where(lane8 == case8, total, 0.0), axis=1, keepdims=True)
        curv = jnp.sum(jnp.where(lane8 == case8 + ROWS, total, 0.0), axis=1, keepdims=True)
        if it == 0:
            ratio = None
            step_size = jnp.where(case_live, rz / jnp.where(case_live, curv, 1.0), 0.0)
        else:
            ratio = jnp.where(case_live, rz / jnp.where(case_live, rz_now, 1.0), 0.0)
            bottom = curv - ratio * rz / jnp.where(case_live, step_size, 1.0)
            step_size = jnp.where(case_live, rz / jnp.where(case_live, bottom, 1.0), 0.0)
        rz_now = rz
        row_live = lax.broadcasted_iota(jnp.int32, (ROWS, LANES), 0) < CASES
        for j in range(J):
            z_j = z_s[it, j]
            y = jnp.where(row_live, img[j], 0.0) + dsh_s[pl.ds(j, 1), :] * z_j
            if j < F:
                y = y + rback[it, 0, j]
            if j >= J - F:
                y = y + rback[it, 1, j - (J - F)]
            if it == 0:
                d_j, a_j = z_j, y
            else:
                d_j = z_j + ratio * d_s[j]
                a_j = y + ratio * al_s[j]
            x_j = x_s[j] + step_size * d_j
            r_j = r_s[j] - step_size * a_j
            if it + 1 < ITERS:
                d_s[j] = d_j
                al_s[j] = a_j
            x_s[j] = x_j
            r_s[j] = r_j

    for source, target in ((x_s, sol_ref), (r_s, res_ref)):
        flat_out = jnp.concatenate([source[j, :, pl.ds(0, BLOCK)] for j in range(J)], axis=1)
        for c in range(CASES):
            target[c] = flat_out[c : c + 1]


def solution(mesh):
    n_slab, n_dom = mesh.shape["slab"], mesh.shape["dom"]
    N = n_slab * n_dom

    def body(rhs, dshift, stiff, face_k, elem_col, elem_row, face_rows):
        span = rhs.shape[2]
        J = span // BLOCK
        E = stiff.shape[1]
        F = face_k.shape[2]
        R = J * n_dom
        H = J // 2
        vmem = pl.BlockSpec(memory_space=pltpu.VMEM)
        anywhere = pl.BlockSpec(memory_space=pl.ANY)
        dma = pltpu.SemaphoreType.DMA
        out = pl.pallas_call(
            functools.partial(kernel, n_slab, n_dom),
            out_shape=(
                pltpu.VMEM((CASES, 1, span), f32),
                pltpu.VMEM((CASES, 1, span), f32),
            ),
            in_specs=[anywhere] * 7,
            out_specs=(vmem, vmem),
            scratch_shapes=[
                pltpu.VMEM((CASES, 1, span), f32),
                pltpu.VMEM((1, span), f32),
                pltpu.VMEM((2, F, BLOCK * BLOCK), bf16),
                pltpu.VMEM((1, E), jnp.int32),
                pltpu.VMEM((1, E), jnp.int32),
                pltpu.SMEM((1, E), jnp.int32),
                pltpu.SMEM((1, E), jnp.int32),
                pltpu.SMEM((1, 2), jnp.int32),
                pltpu.VMEM((E, BLOCK * BLOCK), bf16),
                pltpu.VMEM((SLOTS, 2 * F * 16, LANES), f32),
                pltpu.VMEM((ROWS * GROUP, ROWS * GROUP), bf16),
                pltpu.VMEM((E, BLOCK, LANES), bf16),
                pltpu.VMEM((2 * F, BLOCK, LANES), bf16),
                pltpu.VMEM((PARTS, n_dom, J * ROWS, LANES), f32),
                pltpu.VMEM((E, LANES), f32),
                pltpu.VMEM((J, LANES), f32),
                pltpu.VMEM((J, 2 * ROWS, LANES), bf16),
                pltpu.VMEM((PARTS, R, 2 * ROWS, LANES), bf16),
                pltpu.VMEM((E // ROWS, ROWS, ROWS, LANES), f32),
                pltpu.VMEM((PARTS, E // ROWS, ROWS, ROWS, LANES), f32),
                pltpu.VMEM((J, ROWS, LANES), f32),
                pltpu.VMEM((R, E), bf16),
                pltpu.VMEM((J, E), bf16),
                pltpu.VMEM((J, ROWS, LANES), f32),
                pltpu.VMEM((J, ROWS, LANES), f32),
                pltpu.VMEM((J, ROWS, LANES), f32),
                pltpu.VMEM((J, ROWS, LANES), f32),
                pltpu.VMEM((J, ROWS, LANES), f32),
                pltpu.VMEM((ITERS, J, ROWS, LANES), f32),
                pltpu.VMEM((J, LANES), f32),
                pltpu.VMEM((J, LANES), f32),
                pltpu.VMEM((2, ROWS, LANES), f32),
                pltpu.VMEM((2, ROWS, LANES), f32),
                pltpu.VMEM((ITERS, 2, F, ROWS, LANES), f32),
                pltpu.VMEM((ITERS, PARTS, n_dom, J + H, LANES), f32),
                pltpu.VMEM((ITERS, PARTS, n_dom - 1, J + H, LANES), f32),
                pltpu.VMEM((ITERS, PARTS, n_dom, J + H, LANES), f32),
                pltpu.VMEM((ITERS, 2, F, ROWS, LANES), f32),
                pltpu.VMEM((ITERS, 2, F, ROWS, LANES), f32),
                pltpu.VMEM((ITERS, N, 1, LANES), f32),
                dma((E // CHUNK,)),
                dma((8,)),
                dma((1,)),
                dma((1,)),
                dma((ITERS,)),
                dma((ITERS,)),
                dma((ITERS, PARTS)),
                dma((ITERS, PARTS)),
                dma((ITERS, PARTS)),
                dma((ITERS, PARTS)),
                dma((ITERS,)),
                dma((ITERS,)),
                dma((ITERS,)),
                dma((ITERS,)),
            ],
            compiler_params=pltpu.CompilerParams(
                collective_id=0, has_side_effects=True, vmem_limit_bytes=56 * 1024 * 1024
            ),
        )(
            rhs, dshift, stiff.reshape(E, BLOCK * BLOCK),
            face_k.reshape(2, F, BLOCK * BLOCK), elem_col, elem_row, face_rows,
        )

        def write(sol_v, res_v, sol_o, res_o, sems):
            copies = [
                pltpu.make_async_copy(source, target, sems.at[n])
                for n, (source, target) in enumerate(((sol_v, sol_o), (res_v, res_o)))
            ]
            for c in copies:
                c.start()
            for c in copies:
                c.wait()

        return pl.pallas_call(
            write,
            out_shape=(jax.ShapeDtypeStruct((CASES, 1, span), f32),) * 2,
            in_specs=[vmem, vmem],
            out_specs=(anywhere, anywhere),
            scratch_shapes=[dma((2,))],
        )(*(pltpu.with_memory_space_constraint(x, pltpu.VMEM) for x in out))

    return jax.shard_map(
        body,
        mesh=mesh,
        in_specs=(
            P(None, "slab", "dom"),
            P("slab", "dom"),
            P("slab", "dom", None),
            P("slab", None, "dom", None),
            P("slab", "dom"),
            P("slab", "dom"),
            P("slab", None),
        ),
        out_specs=(P(None, "slab", "dom"), P(None, "slab", "dom")),
        check_vma=False,
    )
```
